32 devices in a mesh: bx: 8 (over z, y), by: 4 (over x, core).
Axes of the slice: x: 2, y: 2, z: 4, core: 2. Of those that a mesh axis runs over, the one named last changes fastest.
Arguments:
- jitter: float32 [8, 4, 2, 256], P('bx', 'by'), may hold values from 0 to 1
- noise_var: float32 [8, 4, 256], P('bx', 'by'), may hold values from 0.5 to 2
- bases: float32 [8, 4, 2, 128, 128], P('bx', 'by'), may hold values from -0.5 to 1.5, as said below
Outputs:
- interior_factor: float32 [8, 4, 128, 128], P('bx', 'by')
- panel: float32 [8, 4, 128, 128], P('bx', 'by')
- couplings: float32 [8, 4, 8, 128, 128], P('bx', 'by')
- parent_factor: float32 [8, 4, 96, 384], P('bx', 'by')
- parent_panel: float32 [8, 4, 96, 128], P('bx', 'by')
- top_factor: float32 [8, 4, 24, 384], P('bx', 'by')
- top_panel: float32 [8, 4, 24, 128], P('bx', 'by')
- top_schur: float32 [8, 4, 8, 128], P('bx', 'by')
The draws below stay inside these ranges and needn't reach their ends.
Inputs may be any that keep to these rules, and one draw needn't show every extreme that they name: `bases`: each of a box's two basis blocks is nonsingular.
All inputs are finite; a program needn't handle non-finite values.
Results may differ from the reference program's by a relative error of at most 0.0003.
Values sent between devices are 32-bit elements; how exact they have to be, the bound alone decides.
A program may use at most 64 MiB of HBM per device.

```python
import functools
import math
import jax
import jax.numpy as jnp
from jax import lax

SKEL = 128
BOX = 256
NBX = 8
NBY = 4


def draw_bases(key, part):
    dims_all = (NBX, NBY, 2, SKEL, SKEL)
    spread_val = 0.25 / SKEL ** 0.5
    perturb = jax.random.normal(key, dims_all, jnp.float32) * spread_val
    return perturb + jnp.eye(SKEL, dtype=jnp.float32)


def levels(stream_key, dims, pieces, least, largest):
    def one(position, blocks):
        heights = jax.random.uniform(jax.random.fold_in(jax.random.fold_in(stream_key, 6), position), (blocks,), jnp.float32, least / len(pieces), largest / len(pieces))
        return jnp.repeat(jnp.exp(heights), dims[position] // blocks).reshape((-1,) + (1,) * (len(dims) - position - 1))

    level = one(*pieces[0])
    for cut in pieces[1:]:
        level = level * one(*cut)
    return level


def setup_inputs(seed: int = 0) -> dict:
    streams_of = jax.random.split(jax.random.key(seed), 4)
    return {
        "jitter": jnp.clip(1.0 * jax.random.uniform(streams_of[0], (NBX, NBY, 2, BOX), jnp.float32) ** levels(streams_of[0], (NBX, NBY, 2, BOX), ((0, 8), (1, 4)), -0.2, 0.2), 0.0, 1.0),
        "noise_var": jnp.clip(jnp.exp(math.log(2.0) - 1.3862944 * jax.random.uniform(streams_of[1], (NBX, NBY, BOX), jnp.float32) ** levels(streams_of[1], (NBX, NBY, BOX), ((0, 8), (1, 4)), -0.2, 0.2)), 0.5, 2.0),
        "bases": draw_bases(jax.random.fold_in(streams_of[3], 71), 0),
    }


RIM = 0.125
OFFSETS = ((-1, -1), (-1, 0), (-1, 1), (0, -1), (0, 1), (1, -1), (1, 0), (1, 1))

def highest(left, right):
    return jnp.dot(left, right, precision=lax.Precision.HIGHEST)

def interior_points(shifts, anchor_x, anchor_y):
    point_total = shifts.shape[-1]
    side_cells = math.isqrt(point_total // 2)
    col_cells = 2 * side_cells
    point_id = jnp.arange(point_total)
    row_id = (point_id // col_cells).astype(jnp.float32)
    col_id = (point_id % col_cells).astype(jnp.float32)
    pitch_rows = (1.0 - 2.0 * RIM) / side_cells
    pitch_cols = (1.0 - 2.0 * RIM) / col_cells
    pos_x = anchor_x + RIM + (row_id + shifts[0]) * pitch_rows
    pos_y = anchor_y + RIM + (col_id + shifts[1]) * pitch_cols
    return (pos_x, pos_y)

def cycle_points(shifts, anchor_x, anchor_y):
    point_total = shifts.shape[-1]
    quarter_count = point_total // 4
    per_layer = point_total // 8
    point_id = jnp.arange(point_total)
    strip_id = point_id // quarter_count
    within_strip = point_id % quarter_count
    layer_id = (within_strip // per_layer).astype(jnp.float32)
    along_pos = ((within_strip % per_layer).astype(jnp.float32) + shifts[0]) / per_layer
    depth_off = (layer_id + shifts[1]) * (0.5 * RIM)
    pos_x = jnp.where(strip_id == 2, depth_off, jnp.where(strip_id == 3, 1.0 - depth_off, along_pos))
    pos_y = jnp.where(strip_id == 0, depth_off, jnp.where(strip_id == 1, 1.0 - depth_off, along_pos))
    return (anchor_x + pos_x, anchor_y + pos_y)

def wendland(first_x, first_y, second_x, second_y):
    gap_x = first_x[:, None] - second_x[None, :]
    gap_y = first_y[:, None] - second_y[None, :]
    radius = jnp.sqrt(gap_x * gap_x + gap_y * gap_y) / RIM
    inside = jnp.maximum(1.0 - radius, 0.0)
    return inside * inside * inside * inside * (4.0 * radius + 1.0)

def box_level(shifts, noise_diag, basis_pair):
    half_box = shifts.shape[-1] // 2
    inner_x, inner_y = interior_points(shifts[:, :half_box], 0.0, 0.0)
    cycle_x, cycle_y = cycle_points(shifts[:, half_box:], 0.0, 0.0)
    kern_inner = wendland(inner_x, inner_y, inner_x, inner_y) + jnp.diag(noise_diag[:half_box])
    kern_mixed = wendland(inner_x, inner_y, cycle_x, cycle_y)
    kern_cycle = wendland(cycle_x, cycle_y, cycle_x, cycle_y) + jnp.diag(noise_diag[half_box:])
    basis_red = basis_pair[0]
    basis_skel = basis_pair[1]
    rot_inner = highest(basis_red.T, highest(kern_inner, basis_red))
    rot_mixed = highest(basis_red.T, highest(kern_mixed, basis_skel))
    rot_cycle = highest(basis_skel.T, highest(kern_cycle, basis_skel))
    lower_tri = jnp.linalg.cholesky(rot_inner)
    panel_rows = jax.scipy.linalg.solve_triangular(lower_tri, rot_mixed, lower=True)
    schur_part = rot_cycle - highest(panel_rows.T, panel_rows)
    return (lower_tri, panel_rows, schur_part, cycle_x, cycle_y)

def coupling(basis_skel, cycle_x, cycle_y, other_basis, other_shifts, shift_x, shift_y):
    other_x, other_y = cycle_points(other_shifts, shift_x, shift_y)
    return highest(basis_skel.T, highest(wendland(cycle_x, cycle_y, other_x, other_y), other_basis))

def coupling_packed(packed, shift_x, shift_y):
    return coupling(packed[0], packed[1], packed[2], packed[3], packed[4], shift_x, shift_y)

def eliminate(matrix):
    block_size = matrix.shape[0] // 4
    kept_count = block_size // 4
    shed_count = block_size - kept_count
    quartet = matrix.reshape(4, block_size, 4, block_size)
    sub_shed = quartet[:, :shed_count, :, :shed_count].reshape(4 * shed_count, 4 * shed_count)
    sub_mixed = quartet[:, :shed_count, :, shed_count:].reshape(4 * shed_count, 4 * kept_count)
    sub_kept = quartet[:, shed_count:, :, shed_count:].reshape(4 * kept_count, 4 * kept_count)
    lower_tri = jnp.linalg.cholesky(sub_shed)
    panel_rows = jax.scipy.linalg.solve_triangular(lower_tri, sub_mixed, lower=True)
    schur_part = sub_kept - highest(panel_rows.T, panel_rows)
    return (lower_tri, panel_rows, schur_part)

def block_at(schur_grid, coupling_grid, step_x, step_y):
    if step_x == 0 and step_y == 0:
        return schur_grid
    return coupling_grid[:, :, OFFSETS.index((step_x, step_y))]

def spread_parent(values, boxes_x, boxes_y):
    row_count = values.shape[1] // 4
    grid_view = values.reshape(boxes_x // 2, boxes_y // 2, 2, 2, row_count, values.shape[2])
    return grid_view.transpose(0, 2, 1, 3, 4, 5).reshape(boxes_x, boxes_y, row_count, values.shape[2])

def spread_grand(values, boxes_x, boxes_y):
    row_count = values.shape[1] // 16
    grid_view = values.reshape(boxes_x // 4, boxes_y // 4, 2, 2, 2, 2, row_count, values.shape[2])
    return grid_view.transpose(0, 2, 4, 1, 3, 5, 6, 7).reshape(boxes_x, boxes_y, row_count, values.shape[2])

def reference(jitter, noise_var, bases):
    boxes_x, boxes_y = (jitter.shape[0], jitter.shape[1])
    half_box = jitter.shape[3] // 2
    kept_count = half_box // 4
    shed_count = half_box - kept_count
    box_total = boxes_x * boxes_y
    flat_jitter = jitter.reshape(box_total, 2, 2 * half_box)
    flat_noise = noise_var.reshape(box_total, 2 * half_box)
    flat_bases = bases.reshape(box_total, 2, half_box, half_box)
    lower_tri, panel_rows, schur_part, cycle_x, cycle_y = lax.map(lambda packed: box_level(packed[0], packed[1], packed[2]), (flat_jitter, flat_noise, flat_bases))
    basis_skel = flat_bases[:, 1]
    pad_shift = jnp.pad(jitter[:, :, :, half_box:], ((1, 1), (1, 1), (0, 0), (0, 0)))
    pad_basis = jnp.pad(bases[:, :, 1], ((1, 1), (1, 1), (0, 0), (0, 0)))
    blocks = []
    for step_x, step_y in OFFSETS:
        other_basis = pad_basis[1 + step_x:1 + step_x + boxes_x, 1 + step_y:1 + step_y + boxes_y]
        other_shift = pad_shift[1 + step_x:1 + step_x + boxes_x, 1 + step_y:1 + step_y + boxes_y]
        mapper = functools.partial(coupling_packed, shift_x=float(step_x), shift_y=float(step_y))
        blocks.append(lax.map(mapper, (basis_skel, cycle_x, cycle_y, other_basis.reshape(box_total, half_box, half_box), other_shift.reshape(box_total, 2, half_box))))
    couplings = jnp.stack(blocks, axis=1).reshape(boxes_x, boxes_y, 8, half_box, half_box)
    schur_grid = schur_part.reshape(boxes_x, boxes_y, half_box, half_box)
    row_blocks = []
    for part_x in (0, 1):
        for part_y in (0, 1):
            col_blocks = []
            for twin_x in (0, 1):
                for twin_y in (0, 1):
                    chosen = block_at(schur_grid, couplings, twin_x - part_x, twin_y - part_y)
                    col_blocks.append(chosen[part_x::2, part_y::2])
            row_blocks.append(jnp.concatenate(col_blocks, axis=3))
    parent_matrix = jnp.concatenate(row_blocks, axis=2)
    parent_total = boxes_x // 2 * (boxes_y // 2)
    parent_lower, parent_panel_all, parent_schur = lax.map(eliminate, parent_matrix.reshape(parent_total, 4 * half_box, 4 * half_box))
    parent_grid = parent_schur.reshape(boxes_x // 2, boxes_y // 2, half_box, half_box)
    grand_x, grand_y = (boxes_x // 4, boxes_y // 4)
    grand_rows = []
    for parent_x in (0, 1):
        for parent_y in (0, 1):
            grand_cols = []
            for other_x in (0, 1):
                for other_y in (0, 1):
                    if parent_x == other_x and parent_y == other_y:
                        grand_cols.append(parent_grid[parent_x::2, parent_y::2])
                        continue
                    sub_rows = []
                    for part_x in (0, 1):
                        for part_y in (0, 1):
                            sub_cols = []
                            for twin_x in (0, 1):
                                for twin_y in (0, 1):
                                    gap_x = 2 * other_x + twin_x - 2 * parent_x - part_x
                                    gap_y = 2 * other_y + twin_y - 2 * parent_y - part_y
                                    if abs(gap_x) <= 1 and abs(gap_y) <= 1:
                                        chosen = couplings[2 * parent_x + part_x::4, 2 * parent_y + part_y::4, OFFSETS.index((gap_x, gap_y)), shed_count:, shed_count:]
                                    else:
                                        chosen = jnp.zeros((grand_x, grand_y, kept_count, kept_count), jnp.float32)
                                    sub_cols.append(chosen)
                            sub_rows.append(jnp.concatenate(sub_cols, axis=3))
                    grand_cols.append(jnp.concatenate(sub_rows, axis=2))
            grand_rows.append(jnp.concatenate(grand_cols, axis=3))
    grand_matrix = jnp.concatenate(grand_rows, axis=2)
    grand_lower, grand_panel, grand_schur = lax.map(eliminate, grand_matrix.reshape(grand_x * grand_y, 4 * half_box, 4 * half_box))
    interior_factor = lower_tri.reshape(boxes_x, boxes_y, half_box, half_box)
    panel = panel_rows.reshape(boxes_x, boxes_y, half_box, half_box)
    parent_factor = spread_parent(parent_lower, boxes_x, boxes_y)
    parent_panel = spread_parent(parent_panel_all, boxes_x, boxes_y)
    top_factor = spread_grand(grand_lower, boxes_x, boxes_y)
    top_panel = spread_grand(grand_panel, boxes_x, boxes_y)
    top_schur = spread_grand(grand_schur, boxes_x, boxes_y)
    return (interior_factor, panel, couplings, parent_factor, parent_panel, top_factor, top_panel, top_schur)
```

```python
import math

import jax
import jax.numpy as jnp
import numpy as np
from jax import lax
from jax.experimental import pallas as pl
from jax.experimental.pallas import tpu as pltpu
from jax.sharding import PartitionSpec as P

RIM = 0.125
OFFSETS = ((-1, -1), (-1, 0), (-1, 1), (0, -1), (0, 1), (1, -1), (1, 0), (1, 1))
PANEL = 64
F32 = jnp.float32


def highest(left, right):
    return jnp.dot(left, right, precision=lax.Precision.HIGHEST, preferred_element_type=F32)


def eliminate_block(block, rhs, panel=PANEL):
    size = block.shape[0]
    rows_a = [block[8 * i : 8 * i + 8] for i in range(size // 8)]
    rows_r = [rhs[8 * i : 8 * i + 8] for i in range(size // 8)]
    sub = lax.broadcasted_iota(jnp.int32, rows_a[0].shape, 0)
    for start in range(0, size, panel):
        stop = min(start + panel, size)
        first, last = start // 8, stop // 8
        for g in range(first, last):
            span = range(g, last)
            cols = {
                (m, i): jnp.broadcast_to(
                    rows_a[i][:, 8 * g + m : 8 * g + m + 1], rows_a[i].shape
                )
                for i in span
                for m in range(8)
            }
            for j in range(8):

                def row(value):
                    return jnp.broadcast_to(value[j : j + 1], value.shape)

                inv = lax.rsqrt(row(cols[j, g]))
                u_a = row(rows_a[g]) * inv
                u_r = row(rows_r[g]) * inv
                u_c = {m: row(cols[m, g]) * inv for m in range(j + 1, 8)}
                for i in span:
                    mult = cols[j, i] * inv
                    for m in range(j + 1, 8):
                        cols[m, i] = cols[m, i] - mult * u_c[m]
                    if i == g:
                        below = jnp.where(sub > j, mult, 0.0)
                        rows_a[i] = jnp.where(sub == j, u_a, rows_a[i] - below * u_a)
                        rows_r[i] = jnp.where(sub == j, u_r, rows_r[i] - below * u_r)
                    else:
                        rows_a[i] = rows_a[i] - mult * u_a
                        rows_r[i] = rows_r[i] - mult * u_r
        if stop < size:
            done_a = jnp.concatenate(rows_a[first:last], axis=0)
            done_r = jnp.concatenate(rows_r[first:last], axis=0)
            change = highest(done_a.T[stop:], jnp.concatenate([done_a, done_r], axis=1))
            for i in range(last, size // 8):
                off = 8 * i - stop
                rows_a[i] = rows_a[i] - change[off : off + 8, :size]
                rows_r[i] = rows_r[i] - change[off : off + 8, size:]
    upper = jnp.concatenate(rows_a, axis=0)
    row_id = lax.broadcasted_iota(jnp.int32, upper.shape, 0)
    col_id = lax.broadcasted_iota(jnp.int32, upper.shape, 1)
    return jnp.where(row_id <= col_id, upper, 0.0), jnp.concatenate(rows_r, axis=0)


def identity(size):
    row_id = lax.broadcasted_iota(jnp.int32, (size, size), 0)
    col_id = lax.broadcasted_iota(jnp.int32, (size, size), 1)
    return jnp.where(row_id == col_id, 1.0, 0.0).astype(F32)


def point_table(count):
    ids = np.arange(count)
    side = 2 * math.isqrt(count // 2)
    within = ids % (count // 4)
    table = np.zeros((8, count), np.float32)
    table[0] = ids // side
    table[1] = ids % side
    table[2] = within % (count // 8)
    table[3] = within // (count // 8)
    table[4] = ids // (count // 4)
    return table


def interior_points(shifts, table):
    side = math.isqrt(shifts.shape[-1] // 2)
    pos_x = RIM + (table[0:1] + shifts[0:1]) * ((1.0 - 2.0 * RIM) / side)
    pos_y = RIM + (table[1:2] + shifts[1:2]) * ((1.0 - 2.0 * RIM) / (2 * side))
    return pos_x, pos_y


def cycle_points(shifts, table):
    along = (table[2:3] + shifts[0:1]) / (shifts.shape[-1] // 8)
    depth = (table[3:4] + shifts[1:2]) * (0.5 * RIM)
    strip = table[4:5]
    pos_x = jnp.where(strip == 2.0, depth, jnp.where(strip == 3.0, 1.0 - depth, along))
    pos_y = jnp.where(strip == 0.0, depth, jnp.where(strip == 1.0, 1.0 - depth, along))
    return pos_x, pos_y


def column(row_value):
    size = row_value.shape[1]
    return jnp.broadcast_to(row_value, (size, size)).T


def wendland(first_x, first_y, second_x, second_y):
    gap_x = first_x - second_x
    gap_y = first_y - second_y
    radius = jnp.sqrt(gap_x * gap_x + gap_y * gap_y) / RIM
    inside = jnp.maximum(1.0 - radius, 0.0)
    return inside * inside * inside * inside * (4.0 * radius + 1.0)


def place():
    return lax.axis_index("bx"), lax.axis_index("by")


def send(source, target, send_sem, recv_sem, device):
    return pltpu.make_async_remote_copy(
        src_ref=source,
        dst_ref=target,
        send_sem=send_sem,
        recv_sem=recv_sem,
        device_id=device,
        device_id_type=pl.DeviceIdType.MESH,
    )


def front_kernel(jitter, noise, bases, table_ref, rotated, near_basis, near_shift, sends, recvs):
    size = bases.shape[-1]
    index_x, index_y = place()
    last_x, last_y = lax.axis_size("bx") - 1, lax.axis_size("by") - 1
    have_x = {0: index_x > 0, 1: index_x >= 0, 2: index_x < last_x}
    have_y = {0: index_y > 0, 2: index_y < last_y}
    count = jnp.int32(0)
    barrier = pltpu.get_barrier_semaphore()
    for i in (0, 2):

        @pl.when(jnp.logical_not(have_x[i]))
        def _():
            near_basis[i] = jnp.zeros(near_basis.shape[1:], F32)
            near_shift[i] = jnp.zeros(near_shift.shape[1:], F32)

        @pl.when(jnp.logical_not(have_y[i]))
        def _():
            near_basis[:, i] = jnp.zeros((3,) + near_basis.shape[2:], F32)
            near_shift[:, i] = jnp.zeros((3,) + near_shift.shape[2:], F32)

    for i in (0, 2):

        @pl.when(have_x[i])
        def _():
            pl.semaphore_signal(barrier, inc=1, device_id=(index_x + i - 1, index_y), device_id_type=pl.DeviceIdType.MESH)

        @pl.when(have_y[i])
        def _():
            pl.semaphore_signal(barrier, inc=1, device_id=(index_x, index_y + i - 1), device_id_type=pl.DeviceIdType.MESH)

        count += have_x[i].astype(jnp.int32) + have_y[i].astype(jnp.int32)
    pl.semaphore_wait(barrier, count)
    own = (bases.at[1], jitter.at[:, size:])
    near = (near_basis, near_shift)

    def along_x(i, part):
        return send(own[part], near[part].at[2 - i, 1], sends.at[0, i, 0, part], recvs.at[2 - i, 1, part], (index_x + i - 1, index_y))

    def along_y(i, k, part):
        source = own[part] if k == 1 else near[part].at[k, 1]
        return send(source, near[part].at[k, 2 - i], sends.at[1, i, k, part], recvs.at[k, 2 - i, part], (index_x, index_y + i - 1))

    def recv_wait(k, i, part):
        slot = near[part].at[k, i]
        send(slot, slot, sends.at[1, i, k, part], recvs.at[k, i, part], (index_x, index_y)).wait_recv()

    for i in (0, 2):

        @pl.when(have_x[i])
        def _():
            for part in (0, 1):
                along_x(i, part).start()

    for i in (0, 2):

        @pl.when(have_y[i])
        def _():
            for part in (0, 1):
                along_y(i, 1, part).start()

    near_basis[1, 1] = bases[1]
    near_shift[1, 1] = jitter[:, size:]
    table = table_ref[...]
    shifts = jitter[...]
    inner_x, inner_y = interior_points(shifts[:, :size], table)
    cycle_x, cycle_y = cycle_points(shifts[:, size:], table)
    inner_cx, inner_cy = column(inner_x), column(inner_y)
    cycle_cx, cycle_cy = column(cycle_x), column(cycle_y)
    eye = identity(size)
    basis_red, basis_skel = bases[0], bases[1]
    red_t, skel_t = basis_red.T, basis_skel.T

    kern_inner = wendland(inner_cx, inner_cy, inner_x, inner_y) + eye * noise[:, :size]
    rotated[0] = highest(red_t, highest(kern_inner, basis_red))
    for k in (0, 2):

        @pl.when(have_x[k])
        def _():
            for part in (0, 1):
                recv_wait(k, 1, part)

        for i in (0, 2):

            @pl.when(have_x[k] & have_y[i])
            def _():
                for part in (0, 1):
                    along_y(i, k, part).start()

    kern_mixed = wendland(inner_cx, inner_cy, cycle_x, cycle_y)
    rotated[1] = highest(red_t, highest(kern_mixed, basis_skel))
    kern_cycle = wendland(cycle_cx, cycle_cy, cycle_x, cycle_y) + eye * noise[:, size:]
    rotated[2] = highest(skel_t, highest(kern_cycle, basis_skel))

    for i in (0, 2):
        for k in (0, 1, 2):

            @pl.when(have_x[k] & have_y[i])
            def _():
                for part in (0, 1):
                    recv_wait(k, i, part)
                    along_y(i, k, part).wait_send()

        @pl.when(have_x[i])
        def _():
            for part in (0, 1):
                along_x(i, part).wait_send()


def box_kernel(rotated, factor, panel, schur):
    upper, rows = eliminate_block(rotated[0], rotated[1])
    factor[...] = upper.T
    panel[...] = rows
    schur[...] = rotated[2] - highest(rows.T, rows)


def flip(index, mask, bit):
    return index + bit * (mask - 2 * mask * (index // mask % 2))


def family(index_x, index_y, p):
    to_x = flip(flip(index_x, 2, p // 8), 1, p // 2 % 2)
    to_y = flip(flip(index_y, 2, p // 4 % 2), 1, p % 2)
    return to_x, to_y


def enter(devices):
    barrier = pltpu.get_barrier_semaphore()
    for device in devices:
        pl.semaphore_signal(barrier, inc=1, device_id=device, device_id_type=pl.DeviceIdType.MESH)
    pl.semaphore_wait(barrier, len(devices))


def coupling_kernel(jitter, bases, table_ref, near_basis, near_shift, schur, couplings, pairs, near, diag, cross, sends, recvs):
    size = bases.shape[-1]
    shed = size - size // 4
    index_x, index_y = place()
    child_x, child_y = index_x % 2, index_y % 2
    own_slot = 2 * child_x + child_y
    other_slot = 2 * (1 - child_x) + child_y
    tile_slot = 2 * (2 * (index_x // 2 % 2) + index_y // 2 % 2) + child_x
    boxes = {p: family(index_x, index_y, p) for p in (1, 2, 4, 6, 8, 10, 12, 14)}
    enter(list(boxes.values()))
    across = send(schur, diag.at[own_slot], sends.at[0], recvs.at[0], boxes[2])
    beside = send(schur, diag.at[own_slot], sends.at[1], recvs.at[1], boxes[1])
    onward = send(diag.at[other_slot], diag.at[other_slot], sends.at[3], recvs.at[3], boxes[1])
    across.start()
    beside.start()
    diag[own_slot] = schur[...]
    table = table_ref[...]
    cycle_x, cycle_y = cycle_points(jitter[:, size:], table)
    column_x, column_y = column(cycle_x), column(cycle_y)
    skel_t = bases[1].T

    def couple(n):
        step_x, step_y = OFFSETS[n]
        other_x, other_y = cycle_points(near_shift[1 + step_x, 1 + step_y], table)
        kern = wendland(column_x, column_y, step_x + other_x, step_y + other_y)
        block = highest(skel_t, highest(kern, near_basis[1 + step_x, 1 + step_y]))
        couplings[n] = block
        return block[shed:, shed:]

    tile = jnp.concatenate([couple(n) for n in range(4, 8)], axis=1)
    cross[...] = tile
    near[tile_slot] = tile
    for n in range(2):
        couple(n)
    tiles = [
        send(cross, near.at[tile_slot], sends.at[p], recvs.at[p], boxes[p])
        for p in (14, 12, 10, 8, 6, 4, 2)
    ]
    for copy in tiles:
        copy.start()
    for n in range(2, 4):
        couple(n)
    across.wait_recv()
    onward.start()
    sources = []
    for slot in range(4):
        at = (1 + slot // 2 - child_x, 1 + slot % 2 - child_y)
        sources.append((near_basis[at],) + cycle_points(near_shift[at], table))
    count = 0
    for slot in range(3):
        basis_t = sources[slot][0].T
        from_x, from_y = column(sources[slot][1]), column(sources[slot][2])
        for other in range(slot + 1, 4):
            basis, to_x, to_y = sources[other]
            step_x, step_y = other // 2 - slot // 2, other % 2 - slot % 2
            kern = wendland(from_x, from_y, step_x + to_x, step_y + to_y)
            pairs[count] = highest(basis_t, highest(kern, basis))
            count += 1
    across.wait_send()
    for copy in [beside, onward] + tiles:
        copy.wait()


def eliminate_large(shed_rows, kept_block, block, lower, panel_rows):
    size = shed_rows.shape[0]
    work = {
        i: shed_rows[i * block : (i + 1) * block, i * block :] for i in range(size // block)
    }
    for k in range(size // block):
        begin, end = k * block, (k + 1) * block
        upper, inverse = eliminate_block(work[k][:, :block], identity(block))
        rest = highest(inverse, work[k][:, block:])
        lower[begin:end, begin:end] = upper.T
        rest_t = rest.T
        for i in range(k + 1, size // block):
            part_t = rest_t[(i - k - 1) * block : (i - k) * block]
            work[i] = work[i] - highest(part_t, rest[:, (i - k - 1) * block :])
            lower[i * block : (i + 1) * block, begin:end] = part_t
            lower[begin:end, i * block : (i + 1) * block] = jnp.zeros((block, block), F32)
        tail = rest[:, size - end :]
        panel_rows[begin:end] = tail
        kept_block = kept_block - highest(rest_t[size - end :], tail)
    return kept_block


def split_rows(grid, shed):
    top = jnp.concatenate(
        [
            jnp.concatenate([b[:shed, :shed] for b in row] + [b[:shed, shed:] for b in row], axis=1)
            for row in grid
        ],
        axis=0,
    )
    kept = jnp.concatenate(
        [jnp.concatenate([b[shed:, shed:] for b in row], axis=1) for row in grid], axis=0
    )
    return top, kept


def parent_kernel(diag, pairs, tiles, factor, panel, upper, near, lower, panel_rows, schur, sends, recvs, local):
    size = pairs.shape[-1]
    shed = size - size // 4
    half = size // 2
    index_x, index_y = place()
    side = index_y % 2
    parent = 2 * (index_x // 2 % 2) + index_y // 2 % 2
    beside = family(index_x, index_y, 1)
    afar = [family(index_x, index_y, p) for p in (12, 8, 4)]
    mine = pltpu.make_async_copy(tiles, near.at[side], local.at[0])
    mine.start()
    enter([beside] + afar)
    onward = [send(tiles, near.at[side], sends.at[3], recvs.at[3], beside)]
    onward[0].start()
    grid = [[None] * 4 for _ in range(4)]
    count = 0
    for slot in range(4):
        grid[slot][slot] = diag[slot]
        for other in range(slot + 1, 4):
            grid[slot][other] = pairs[count]
            grid[other][slot] = pairs[count].T
            count += 1
    rows, kept = split_rows(grid, shed)
    result = eliminate_large(rows, kept, size, lower, panel_rows)
    schur[...] = result
    upper[parent] = result
    rows = pl.ds(pl.multiple_of(side * half, 8), half)
    out = [
        send(schur.at[rows], upper.at[parent, rows], sends.at[p], recvs.at[p], device)
        for p, device in enumerate(afar)
    ]
    for copy in out:
        copy.start()
    own = pl.ds(pl.multiple_of((2 * (index_x % 2) + index_y % 2) * shed, 8), shed)
    factor[...] = lower[own, :]
    panel[...] = panel_rows[own, :]
    for p in range(3):
        other = (
            2 * ((index_x // 2 + (1, 1, 0)[p]) % 2) + (index_y // 2 + (1, 0, 1)[p]) % 2
        )
        out[p].wait_recv()
        block = upper.at[other, rows]
        onward.append(send(block, block, sends.at[4 + p], recvs.at[4 + p], beside))
        onward[-1].start()
    for copy in [mine] + onward:
        copy.wait()
    for copy in out:
        copy.wait_send()


def grand_kernel(diag, near, factor, panel, schur, lower, panel_rows, kept_rows):
    size = diag.shape[-1]
    kept_size = size // 4
    shed = size - kept_size
    empty = jnp.zeros((kept_size, kept_size), F32)
    tiles = [near[g % 2, g // 2] for g in range(16)]
    turned = [tile.T for tile in tiles]

    def piece(e, c, f, d):
        gap_x = 2 * (f // 2 - e // 2) + d // 2 - c // 2
        gap_y = 2 * (f % 2 - e % 2) + d % 2 - c % 2
        if (gap_x, gap_y) in OFFSETS[4:]:
            at = OFFSETS[4:].index((gap_x, gap_y)) * kept_size
            return tiles[4 * e + c][:, at : at + kept_size]
        if (-gap_x, -gap_y) in OFFSETS[4:]:
            at = OFFSETS[4:].index((-gap_x, -gap_y)) * kept_size
            return turned[4 * f + d][at : at + kept_size]
        return empty

    grid = [[None] * 4 for _ in range(4)]
    for e in range(4):
        grid[e][e] = diag[e]
        for f in range(e + 1, 4):
            grid[e][f] = jnp.concatenate(
                [
                    jnp.concatenate([piece(e, c, f, d) for d in range(4)], axis=1)
                    for c in range(4)
                ],
                axis=0,
            )
            grid[f][e] = grid[e][f].T
    rows, kept = split_rows(grid, shed)
    kept_rows[...] = eliminate_large(rows, kept, size, lower, panel_rows)
    index_x, index_y = place()
    parent = 2 * (index_x // 2 % 2) + index_y // 2 % 2
    slot = 4 * parent + 2 * (index_x % 2) + index_y % 2

    def own(count):
        return pl.ds(pl.multiple_of(slot * count, 8), count)

    factor[...] = lower[own(shed // 4), :]
    panel[...] = panel_rows[own(shed // 4), :]
    schur[...] = kept_rows[own(size // 16), :]


def call(body, shapes, args, name, scratch=(), group=None):
    return pl.pallas_call(
        body,
        out_shape=[jax.ShapeDtypeStruct(s, F32) for s in shapes],
        in_specs=[pl.BlockSpec(memory_space=pltpu.VMEM)] * len(args),
        out_specs=[pl.BlockSpec(memory_space=pltpu.VMEM)] * len(shapes),
        scratch_shapes=[
            pltpu.SemaphoreType.DMA(s[1:]) if s[0] == 0 else pltpu.VMEM(s, F32) for s in scratch
        ],
        compiler_params=pltpu.CompilerParams(
            vmem_limit_bytes=48 * 2**20,
            collective_id=group,
            has_side_effects=group is not None,
        ),
        name=name,
    )(*args)


def on_device(jitter, noise_var, bases):
    jitter, noise, bases = jitter[0, 0], noise_var[0], bases[0, 0]
    size = bases.shape[-1]
    kept = size // 4
    shed = size - kept
    table = jnp.asarray(point_table(size))
    square = (size, size)
    rotated, near_basis, near_shift = call(
        front_kernel,
        [(3,) + square, (3, 3) + square, (3, 3, 2, size)],
        (jitter, noise, bases, table),
        "front",
        [(0, 2, 3, 3, 2), (0, 3, 3, 2)],
        group=0,
    )
    factor, panel, schur = call(box_kernel, [square] * 3, (rotated,), "box")
    couplings, pairs, tiles, quartet = call(
        coupling_kernel,
        [(8,) + square, (6,) + square, (8, kept, size), (4,) + square],
        (jitter, bases, table, near_basis, near_shift, schur),
        "coupling",
        [(kept, size), (0, 15), (0, 15)],
        group=1,
    )
    wide = 4 * shed
    parent_factor, parent_panel, upper, near = call(
        parent_kernel,
        [(shed, wide), (shed, size), (4,) + square, (2, 8, kept, size)],
        (quartet, pairs, tiles),
        "parent",
        [(wide, wide), (wide, size), square, (0, 7), (0, 7), (0, 1)],
        group=2,
    )
    top_factor, top_panel, top_schur = call(
        grand_kernel,
        [(shed // 4, wide), (shed // 4, size), (size // 16, size)],
        (upper, near),
        "grand",
        [(wide, wide), (wide, size), square],
    )
    outs = (
        factor,
        panel,
        couplings,
        parent_factor,
        parent_panel,
        top_factor,
        top_panel,
        top_schur,
    )
    return tuple(value[None, None] for value in outs)


def solution(mesh):
    spec4 = P("bx", "by", None, None)
    spec5 = P("bx", "by", None, None, None)
    return jax.shard_map(
        on_device,
        mesh=mesh,
        in_specs=(spec4, P("bx", "by", None), spec5),
        out_specs=(spec4, spec4, spec5, spec4, spec4, spec4, spec4, spec4),
        check_vma=False,
    )
```

```python
import math

import jax
import jax.numpy as jnp
import numpy as np
from jax import lax
from jax.experimental import pallas as pl
from jax.experimental.pallas import tpu as pltpu
from jax.sharding import PartitionSpec as P

RIM = 0.125
OFFSETS = ((-1, -1), (-1, 0), (-1, 1), (0, -1), (0, 1), (1, -1), (1, 0), (1, 1))
PANEL = 16
F32 = jnp.float32
BF16 = jnp.bfloat16


def highest(left, right):
    return jnp.dot(left, right, precision=lax.Precision.HIGHEST, preferred_element_type=F32)


def pieces(value):
    high = value.astype(BF16)
    rest = value - high.astype(F32)
    middle = rest.astype(BF16)
    return high, middle, (rest - middle.astype(F32)).astype(BF16)


def joined(left, right, left_axis):
    lh, lm, ll = pieces(left)
    rh, rm, rl = pieces(right)
    lefts = jnp.concatenate([lh, lh, lm, lm, lh, ll], axis=left_axis)
    rights = jnp.concatenate([rh, rm, rh, rm, rl, rh], axis=0)
    return (lefts if left_axis else lefts.T), rights


def precise(left, right):
    lefts, rights = joined(left, right, 1)
    return jnp.dot(lefts, rights, preferred_element_type=F32)


def precise_t(left_t, right):
    lefts, rights = joined(left_t, right, 0)
    return jnp.dot(lefts, rights, preferred_element_type=F32)


def lane_copy(value, at):
    return jnp.take_along_axis(
        value, jnp.full(value.shape, at, jnp.int32), axis=1, mode="promise_in_bounds"
    )


def factor_block(block, panel=PANEL):
    size = block.shape[0]
    rows = [block[8 * i : 8 * i + 8] for i in range(size // 8)]
    sub = lax.broadcasted_iota(jnp.int32, rows[0].shape, 0)
    lane = lax.broadcasted_iota(jnp.int32, rows[0].shape, 1)
    uppers, diags = [], []
    for start in range(0, size, panel):
        stop = min(start + panel, size)
        first, last = start // 8, stop // 8
        for g in range(first, last):
            span = range(g, last)
            cols = {(m, i): lane_copy(rows[i], 8 * g + m) for i in span for m in range(8)}
            here = (lane >= 8 * g) & (lane < 8 * g + 8)
            unit = jnp.where(sub == lane - 8 * g, 1.0, 0.0)
            for i in span:
                rows[i] = jnp.where(here, unit if i == g else 0.0, rows[i])
            diag = jnp.zeros_like(rows[g])
            for j in range(8):

                def row(value):
                    return jnp.broadcast_to(value[j : j + 1], value.shape)

                inv = lax.rsqrt(row(cols[j, g]))
                u_c = {m: row(cols[m, g]) * inv for m in range(j + 1, 8)}
                mults = {}
                for i in span:
                    mults[i] = cols[j, i] * inv
                    for m in range(j + 1, 8):
                        cols[m, i] = cols[m, i] - mults[i] * u_c[m]
                u = row(rows[g]) * inv
                diag = jnp.where((lane == 8 * g + j) & (sub >= j), mults[g], diag)
                below = jnp.where(sub > j, mults[g], 0.0)
                rows[g] = jnp.where(sub == j, u, rows[g] - below * u)
                for i in span[1:]:
                    rows[i] = rows[i] - mults[i] * u
            diags.append(diag)
            uppers.append(jnp.where(lane >= 8 * g + 8, rows[g], 0.0))
        if stop < size:
            kept = [
                jnp.where((lane >= 8 * g + 8) & (lane < stop), 0.0, rows[g])
                for g in range(first, last)
            ]
            change = precise_t(
                jnp.concatenate(uppers[first:last], axis=0), jnp.concatenate(kept, axis=0)
            )
            gone = (lane >= start) & (lane < stop)
            for i in range(last, size // 8):
                rows[i] = jnp.where(gone, 0.0, rows[i]) - change[8 * i : 8 * i + 8]
    lower = jnp.concatenate(uppers, axis=0).T + jnp.concatenate(diags, axis=0)
    full = jnp.concatenate(rows, axis=0)
    row_id = lax.broadcasted_iota(jnp.int32, full.shape, 0)
    col_id = lax.broadcasted_iota(jnp.int32, full.shape, 1)
    return lower, jnp.where(col_id < row_id // 8 * 8 + 8, full, 0.0)


def identity(size):
    row_id = lax.broadcasted_iota(jnp.int32, (size, size), 0)
    col_id = lax.broadcasted_iota(jnp.int32, (size, size), 1)
    return jnp.where(row_id == col_id, 1.0, 0.0).astype(F32)


def point_table(count):
    ids = np.arange(count)
    side = 2 * math.isqrt(count // 2)
    within = ids % (count // 4)
    table = np.zeros((8, count), np.float32)
    table[0] = ids // side
    table[1] = ids % side
    table[2] = within % (count // 8)
    table[3] = within // (count // 8)
    table[4] = ids // (count // 4)
    return table


def interior_points(shifts, table):
    side = math.isqrt(shifts.shape[-1] // 2)
    pos_x = RIM + (table[0:1] + shifts[0:1]) * ((1.0 - 2.0 * RIM) / side)
    pos_y = RIM + (table[1:2] + shifts[1:2]) * ((1.0 - 2.0 * RIM) / (2 * side))
    return pos_x, pos_y


def cycle_points(shifts, table):
    along = (table[2:3] + shifts[0:1]) / (shifts.shape[-1] // 8)
    depth = (table[3:4] + shifts[1:2]) * (0.5 * RIM)
    strip = table[4:5]
    pos_x = jnp.where(strip == 2.0, depth, jnp.where(strip == 3.0, 1.0 - depth, along))
    pos_y = jnp.where(strip == 0.0, depth, jnp.where(strip == 1.0, 1.0 - depth, along))
    return pos_x, pos_y


def column(row_value):
    size = row_value.shape[1]
    return jnp.broadcast_to(row_value, (size, size)).T


def wendland(first_x, first_y, second_x, second_y):
    gap_x = first_x - second_x
    gap_y = first_y - second_y
    radius = jnp.sqrt(gap_x * gap_x + gap_y * gap_y) / RIM
    inside = jnp.maximum(1.0 - radius, 0.0)
    return inside * inside * inside * inside * (4.0 * radius + 1.0)


def place():
    return lax.axis_index("bx"), lax.axis_index("by")


def send(source, target, send_sem, recv_sem, device):
    return pltpu.make_async_remote_copy(
        src_ref=source,
        dst_ref=target,
        send_sem=send_sem,
        recv_sem=recv_sem,
        device_id=device,
        device_id_type=pl.DeviceIdType.MESH,
    )


def front_kernel(jitter, noise, bases, table_ref, rotated, near_basis, near_shift, sends, recvs):
    size = bases.shape[-1]
    index_x, index_y = place()
    last_x, last_y = lax.axis_size("bx") - 1, lax.axis_size("by") - 1
    have_x = {0: index_x > 0, 1: index_x >= 0, 2: index_x < last_x}
    have_y = {0: index_y > 0, 2: index_y < last_y}
    count = jnp.int32(0)
    barrier = pltpu.get_barrier_semaphore()
    for i in (0, 2):

        @pl.when(jnp.logical_not(have_x[i]))
        def _():
            near_basis[i] = jnp.zeros(near_basis.shape[1:], F32)
            near_shift[i] = jnp.zeros(near_shift.shape[1:], F32)

        @pl.when(jnp.logical_not(have_y[i]))
        def _():
            near_basis[:, i] = jnp.zeros((3,) + near_basis.shape[2:], F32)
            near_shift[:, i] = jnp.zeros((3,) + near_shift.shape[2:], F32)

    for i in (0, 2):

        @pl.when(have_x[i])
        def _():
            pl.semaphore_signal(barrier, inc=1, device_id=(index_x + i - 1, index_y), device_id_type=pl.DeviceIdType.MESH)

        @pl.when(have_y[i])
        def _():
            pl.semaphore_signal(barrier, inc=1, device_id=(index_x, index_y + i - 1), device_id_type=pl.DeviceIdType.MESH)

        count += have_x[i].astype(jnp.int32) + have_y[i].astype(jnp.int32)
    pl.semaphore_wait(barrier, count)
    own = (bases.at[1], jitter.at[:, size:])
    near = (near_basis, near_shift)

    def along_x(i, part):
        return send(own[part], near[part].at[2 - i, 1], sends.at[0, i, 0, part], recvs.at[2 - i, 1, part], (index_x + i - 1, index_y))

    def along_y(i, k, part):
        source = own[part] if k == 1 else near[part].at[k, 1]
        return send(source, near[part].at[k, 2 - i], sends.at[1, i, k, part], recvs.at[k, 2 - i, part], (index_x, index_y + i - 1))

    def recv_wait(k, i, part):
        slot = near[part].at[k, i]
        send(slot, slot, sends.at[1, i, k, part], recvs.at[k, i, part], (index_x, index_y)).wait_recv()

    for i in (0, 2):

        @pl.when(have_x[i])
        def _():
            for part in (0, 1):
                along_x(i, part).start()

    for i in (0, 2):

        @pl.when(have_y[i])
        def _():
            for part in (0, 1):
                along_y(i, 1, part).start()

    near_basis[1, 1] = bases[1]
    near_shift[1, 1] = jitter[:, size:]
    table = table_ref[...]
    shifts = jitter[...]
    inner_x, inner_y = interior_points(shifts[:, :size], table)
    cycle_x, cycle_y = cycle_points(shifts[:, size:], table)
    inner_cx, inner_cy = column(inner_x), column(inner_y)
    cycle_cx, cycle_cy = column(cycle_x), column(cycle_y)
    eye = identity(size)
    basis_red, basis_skel = bases[0], bases[1]
    red_t, skel_t = basis_red.T, basis_skel.T

    kern_inner = wendland(inner_cx, inner_cy, inner_x, inner_y) + eye * noise[:, :size]
    rotated[0] = highest(red_t, highest(kern_inner, basis_red))
    for k in (0, 2):

        @pl.when(have_x[k])
        def _():
            for part in (0, 1):
                recv_wait(k, 1, part)

        for i in (0, 2):

            @pl.when(have_x[k] & have_y[i])
            def _():
                for part in (0, 1):
                    along_y(i, k, part).start()

    kern_mixed = wendland(inner_cx, inner_cy, cycle_x, cycle_y)
    rotated[1] = highest(red_t, highest(kern_mixed, basis_skel))
    kern_cycle = wendland(cycle_cx, cycle_cy, cycle_x, cycle_y) + eye * noise[:, size:]
    rotated[2] = highest(skel_t, highest(kern_cycle, basis_skel))

    for i in (0, 2):
        for k in (0, 1, 2):

            @pl.when(have_x[k] & have_y[i])
            def _():
                for part in (0, 1):
                    recv_wait(k, i, part)
                    along_y(i, k, part).wait_send()

        @pl.when(have_x[i])
        def _():
            for part in (0, 1):
                along_x(i, part).wait_send()


def box_kernel(rotated, factor, panel, schur):
    lower, inverse = factor_block(rotated[0])
    rows = precise(inverse, rotated[1])
    factor[...] = lower
    panel[...] = rows
    schur[...] = rotated[2] - precise(rows.T, rows)


def flip(index, mask, bit):
    return index + bit * (mask - 2 * mask * (index // mask % 2))


def family(index_x, index_y, p):
    to_x = flip(flip(index_x, 2, p // 8), 1, p // 2 % 2)
    to_y = flip(flip(index_y, 2, p // 4 % 2), 1, p % 2)
    return to_x, to_y


def enter(devices):
    barrier = pltpu.get_barrier_semaphore()
    for device in devices:
        pl.semaphore_signal(barrier, inc=1, device_id=device, device_id_type=pl.DeviceIdType.MESH)
    pl.semaphore_wait(barrier, len(devices))


def coupling_kernel(jitter, bases, table_ref, near_basis, near_shift, schur, couplings, pairs, near, diag, cross, sends, recvs):
    size = bases.shape[-1]
    shed = size - size // 4
    index_x, index_y = place()
    child_x, child_y = index_x % 2, index_y % 2
    own_slot = 2 * child_x + child_y
    other_slot = 2 * (1 - child_x) + child_y
    tile_slot = 2 * (2 * (index_x // 2 % 2) + index_y // 2 % 2) + child_x
    boxes = {p: family(index_x, index_y, p) for p in (1, 2, 4, 6, 8, 10, 12, 14)}
    enter(list(boxes.values()))
    across = send(schur, diag.at[own_slot], sends.at[0], recvs.at[0], boxes[2])
    beside = send(schur, diag.at[own_slot], sends.at[1], recvs.at[1], boxes[1])
    onward = send(diag.at[other_slot], diag.at[other_slot], sends.at[3], recvs.at[3], boxes[1])
    across.start()
    beside.start()
    diag[own_slot] = schur[...]
    table = table_ref[...]
    cycle_x, cycle_y = cycle_points(jitter[:, size:], table)
    column_x, column_y = column(cycle_x), column(cycle_y)
    skel_t = bases[1].T

    def couple(n):
        step_x, step_y = OFFSETS[n]
        other_x, other_y = cycle_points(near_shift[1 + step_x, 1 + step_y], table)
        kern = wendland(column_x, column_y, step_x + other_x, step_y + other_y)
        block = highest(skel_t, highest(kern, near_basis[1 + step_x, 1 + step_y]))
        couplings[n] = block
        return block[shed:, shed:]

    tile = jnp.concatenate([couple(n) for n in range(4, 8)], axis=1)
    cross[...] = tile
    near[tile_slot] = tile
    for n in range(2):
        couple(n)
    tiles = [
        send(cross, near.at[tile_slot], sends.at[p], recvs.at[p], boxes[p])
        for p in (14, 12, 10, 8, 6, 4, 2)
    ]
    for copy in tiles:
        copy.start()
    for n in range(2, 4):
        couple(n)
    across.wait_recv()
    onward.start()
    sources = []
    for slot in range(4):
        at = (1 + slot // 2 - child_x, 1 + slot % 2 - child_y)
        sources.append((near_basis[at],) + cycle_points(near_shift[at], table))
    count = 0
    for slot in range(3):
        basis_t = sources[slot][0].T
        from_x, from_y = column(sources[slot][1]), column(sources[slot][2])
        for other in range(slot + 1, 4):
            basis, to_x, to_y = sources[other]
            step_x, step_y = other // 2 - slot // 2, other % 2 - slot % 2
            kern = wendland(from_x, from_y, step_x + to_x, step_y + to_y)
            pairs[count] = highest(basis_t, highest(kern, basis))
            count += 1
    across.wait_send()
    for copy in [beside, onward] + tiles:
        copy.wait()


def gather_kernel(schur, tiles, diag, near, sends, recvs, local):
    size = schur.shape[0]
    half = size // 2
    index_x, index_y = place()
    side = index_y % 2
    parent = 2 * (index_x // 2 % 2) + index_y // 2 % 2
    beside = family(index_x, index_y, 1)
    afar = [family(index_x, index_y, p) for p in (12, 8, 4)]
    mine = [
        pltpu.make_async_copy(schur, diag.at[parent], local.at[0]),
        pltpu.make_async_copy(tiles, near.at[side], local.at[1]),
    ]
    for copy in mine:
        copy.start()
    enter([beside] + afar)
    rows = pl.ds(pl.multiple_of(side * half, 8), half)
    out = [
        send(schur.at[rows], diag.at[parent, rows], sends.at[p], recvs.at[p], device)
        for p, device in enumerate(afar)
    ]
    for copy in out:
        copy.start()
    onward = [send(tiles, near.at[side], sends.at[3], recvs.at[3], beside)]
    onward[0].start()
    for p in range(3):
        other = (
            2 * ((index_x // 2 + (1, 1, 0)[p]) % 2) + (index_y // 2 + (1, 0, 1)[p]) % 2
        )
        out[p].wait_recv()
        block = diag.at[other, rows]
        onward.append(send(block, block, sends.at[4 + p], recvs.at[4 + p], beside))
        onward[-1].start()
    for copy in mine + onward:
        copy.wait()
    for copy in out:
        copy.wait_send()


def eliminate_large(shed_rows, kept_block, block, lower, panel_rows):
    size = shed_rows.shape[0]
    work = {
        i: shed_rows[i * block : (i + 1) * block, i * block :] for i in range(size // block)
    }
    for k in range(size // block):
        begin, end = k * block, (k + 1) * block
        factor, inverse = factor_block(work[k][:, :block])
        rest = precise(inverse, work[k][:, block:])
        lower[begin:end, begin:end] = factor
        rest_t = rest.T
        for i in range(k + 1, size // block):
            part_t = rest_t[(i - k - 1) * block : (i - k) * block]
            work[i] = work[i] - precise(part_t, rest[:, (i - k - 1) * block :])
            lower[i * block : (i + 1) * block, begin:end] = part_t
            lower[begin:end, i * block : (i + 1) * block] = jnp.zeros((block, block), F32)
        tail = rest[:, size - end :]
        panel_rows[begin:end] = tail
        kept_block = kept_block - precise(rest_t[size - end :], tail)
    return kept_block


def split_rows(grid, shed):
    top = jnp.concatenate(
        [
            jnp.concatenate([b[:shed, :shed] for b in row] + [b[:shed, shed:] for b in row], axis=1)
            for row in grid
        ],
        axis=0,
    )
    kept = jnp.concatenate(
        [jnp.concatenate([b[shed:, shed:] for b in row], axis=1) for row in grid], axis=0
    )
    return top, kept


def parent_kernel(diag, pairs, factor, panel, schur, lower, panel_rows):
    size = pairs.shape[-1]
    shed = size - size // 4
    grid = [[None] * 4 for _ in range(4)]
    count = 0
    for slot in range(4):
        grid[slot][slot] = diag[slot]
        for other in range(slot + 1, 4):
            grid[slot][other] = pairs[count]
            grid[other][slot] = pairs[count].T
            count += 1
    rows, kept = split_rows(grid, shed)
    schur[...] = eliminate_large(rows, kept, size, lower, panel_rows)
    index_x, index_y = place()
    own = pl.ds(pl.multiple_of((2 * (index_x % 2) + index_y % 2) * shed, 8), shed)
    factor[...] = lower[own, :]
    panel[...] = panel_rows[own, :]


def grand_kernel(diag, near, factor, panel, schur, lower, panel_rows, kept_rows):
    size = diag.shape[-1]
    kept_size = size // 4
    shed = size - kept_size
    empty = jnp.zeros((kept_size, kept_size), F32)
    tiles = [near[g % 2, g // 2] for g in range(16)]
    turned = [tile.T for tile in tiles]

    def piece(e, c, f, d):
        gap_x = 2 * (f // 2 - e // 2) + d // 2 - c // 2
        gap_y = 2 * (f % 2 - e % 2) + d % 2 - c % 2
        if (gap_x, gap_y) in OFFSETS[4:]:
            at = OFFSETS[4:].index((gap_x, gap_y)) * kept_size
            return tiles[4 * e + c][:, at : at + kept_size]
        if (-gap_x, -gap_y) in OFFSETS[4:]:
            at = OFFSETS[4:].index((-gap_x, -gap_y)) * kept_size
            return turned[4 * f + d][at : at + kept_size]
        return empty

    grid = [[None] * 4 for _ in range(4)]
    for e in range(4):
        grid[e][e] = diag[e]
        for f in range(e + 1, 4):
            grid[e][f] = jnp.concatenate(
                [
                    jnp.concatenate([piece(e, c, f, d) for d in range(4)], axis=1)
                    for c in range(4)
                ],
                axis=0,
            )
            grid[f][e] = grid[e][f].T
    rows, kept = split_rows(grid, shed)
    kept_rows[...] = eliminate_large(rows, kept, size, lower, panel_rows)
    index_x, index_y = place()
    parent = 2 * (index_x // 2 % 2) + index_y // 2 % 2
    slot = 4 * parent + 2 * (index_x % 2) + index_y % 2

    def own(count):
        return pl.ds(pl.multiple_of(slot * count, 8), count)

    factor[...] = lower[own(shed // 4), :]
    panel[...] = panel_rows[own(shed // 4), :]
    schur[...] = kept_rows[own(size // 16), :]


def call(body, shapes, args, name, scratch=(), group=None):
    return pl.pallas_call(
        body,
        out_shape=[jax.ShapeDtypeStruct(s, F32) for s in shapes],
        in_specs=[pl.BlockSpec(memory_space=pltpu.VMEM)] * len(args),
        out_specs=[pl.BlockSpec(memory_space=pltpu.VMEM)] * len(shapes),
        scratch_shapes=[
            pltpu.SemaphoreType.DMA(s[1:]) if s[0] == 0 else pltpu.VMEM(s, F32) for s in scratch
        ],
        compiler_params=pltpu.CompilerParams(
            vmem_limit_bytes=48 * 2**20,
            collective_id=group,
            has_side_effects=group is not None,
        ),
        name=name,
    )(*args)


def on_device(jitter, noise_var, bases):
    jitter, noise, bases = jitter[0, 0], noise_var[0], bases[0, 0]
    size = bases.shape[-1]
    kept = size // 4
    shed = size - kept
    table = jnp.asarray(point_table(size))
    square = (size, size)
    rotated, near_basis, near_shift = call(
        front_kernel,
        [(3,) + square, (3, 3) + square, (3, 3, 2, size)],
        (jitter, noise, bases, table),
        "front",
        [(0, 2, 3, 3, 2), (0, 3, 3, 2)],
        group=0,
    )
    factor, panel, schur = call(box_kernel, [square] * 3, (rotated,), "box")
    couplings, pairs, tiles, quartet = call(
        coupling_kernel,
        [(8,) + square, (6,) + square, (8, kept, size), (4,) + square],
        (jitter, bases, table, near_basis, near_shift, schur),
        "coupling",
        [(kept, size), (0, 15), (0, 15)],
        group=1,
    )
    wide = 4 * shed
    parent_factor, parent_panel, parent_schur = call(
        parent_kernel,
        [(shed, wide), (shed, size), square],
        (quartet, pairs),
        "parent",
        [(wide, wide), (wide, size)],
    )
    upper, near = call(
        gather_kernel,
        [(4,) + square, (2, 8, kept, size)],
        (parent_schur, tiles),
        "gather",
        [(0, 7), (0, 7), (0, 2)],
        group=2,
    )
    top_factor, top_panel, top_schur = call(
        grand_kernel,
        [(shed // 4, wide), (shed // 4, size), (size // 16, size)],
        (upper, near),
        "grand",
        [(wide, wide), (wide, size), square],
    )
    outs = (
        factor,
        panel,
        couplings,
        parent_factor,
        parent_panel,
        top_factor,
        top_panel,
        top_schur,
    )
    return tuple(value[None, None] for value in outs)


def solution(mesh):
    spec4 = P("bx", "by", None, None)
    spec5 = P("bx", "by", None, None, None)
    return jax.shard_map(
        on_device,
        mesh=mesh,
        in_specs=(spec4, P("bx", "by", None), spec5),
        out_specs=(spec4, spec4, spec5, spec4, spec4, spec4, spec4, spec4),
        check_vma=False,
    )
```

```python
import math

import jax
import jax.numpy as jnp
from jax import lax
from jax.experimental import pallas as pl
from jax.experimental.pallas import tpu as pltpu
from jax.sharding import PartitionSpec as P

RIM = 0.125
OFFSETS = ((-1, -1), (-1, 0), (-1, 1), (0, -1), (0, 1), (1, -1), (1, 0), (1, 1))
PANEL = 64
F32 = jnp.float32
BF16 = jnp.bfloat16


def pieces(value):
    high = value.astype(BF16)
    rest = value - high.astype(F32)
    middle = rest.astype(BF16)
    return high, middle, (rest - middle.astype(F32)).astype(BF16)


def joined(left, right, left_axis):
    lh, lm, ll = pieces(left)
    rh, rm, rl = pieces(right)
    lefts = jnp.concatenate([lh, lh, lm, lm, lh, ll], axis=left_axis)
    rights = jnp.concatenate([rh, rm, rh, rm, rl, rh], axis=0)
    return (lefts if left_axis else lefts.T), rights


def precise(left, right):
    lefts, rights = joined(left, right, 1)
    return jnp.dot(lefts, rights, preferred_element_type=F32)


def precise_t(left_t, right):
    lefts, rights = joined(left_t, right, 0)
    return jnp.dot(lefts, rights, preferred_element_type=F32)


def lane_copy(value, at):
    return jnp.take_along_axis(
        value, jnp.full(value.shape, at, jnp.int32), axis=1, mode="promise_in_bounds"
    )


def factor_block(block, panel=PANEL):
    size = block.shape[0]
    rows = [block[8 * i : 8 * i + 8] for i in range(size // 8)]
    sub = lax.broadcasted_iota(jnp.int32, rows[0].shape, 0)
    lane = lax.broadcasted_iota(jnp.int32, rows[0].shape, 1)
    uppers, diags = [], []
    for start in range(0, size, panel):
        stop = min(start + panel, size)
        first, last = start // 8, stop // 8
        for g in range(first, last):
            span = range(g, last)
            cols = {(m, i): lane_copy(rows[i], 8 * g + m) for i in span for m in range(8)}
            here = (lane >= 8 * g) & (lane < 8 * g + 8)
            unit = jnp.where(sub == lane - 8 * g, 1.0, 0.0)
            for i in span:
                rows[i] = jnp.where(here, unit if i == g else 0.0, rows[i])
            diag = jnp.zeros_like(rows[g])
            for j in range(8):

                def row(value):
                    return jnp.broadcast_to(value[j : j + 1], value.shape)

                inv = lax.rsqrt(row(cols[j, g]))
                u_c = {m: row(cols[m, g]) * inv for m in range(j + 1, 8)}
                mults = {}
                for i in span:
                    mults[i] = cols[j, i] * inv
                    for m in range(j + 1, 8):
                        cols[m, i] = cols[m, i] - mults[i] * u_c[m]
                u = row(rows[g]) * inv
                diag = jnp.where((lane == 8 * g + j) & (sub >= j), mults[g], diag)
                below = jnp.where(sub > j, mults[g], 0.0)
                rows[g] = jnp.where(sub == j, u, rows[g] - below * u)
                for i in span[1:]:
                    rows[i] = rows[i] - mults[i] * u
            diags.append(diag)
            uppers.append(jnp.where(lane >= 8 * g + 8, rows[g], 0.0))
        if stop < size:
            kept = [
                jnp.where((lane >= 8 * g + 8) & (lane < stop), 0.0, rows[g])
                for g in range(first, last)
            ]
            change = precise_t(
                jnp.concatenate(uppers[first:last], axis=0), jnp.concatenate(kept, axis=0)
            )
            gone = (lane >= start) & (lane < stop)
            for i in range(last, size // 8):
                rows[i] = jnp.where(gone, 0.0, rows[i]) - change[8 * i : 8 * i + 8]
    lower = jnp.concatenate(uppers, axis=0).T + jnp.concatenate(diags, axis=0)
    full = jnp.concatenate(rows, axis=0)
    row_id = lax.broadcasted_iota(jnp.int32, full.shape, 0)
    col_id = lax.broadcasted_iota(jnp.int32, full.shape, 1)
    return lower, jnp.where(col_id < row_id // 8 * 8 + 8, full, 0.0)


def identity(size):
    row_id = lax.broadcasted_iota(jnp.int32, (size, size), 0)
    col_id = lax.broadcasted_iota(jnp.int32, (size, size), 1)
    return jnp.where(row_id == col_id, 1.0, 0.0).astype(F32)


def point_table(count):
    ids = lax.broadcasted_iota(jnp.int32, (1, count), 1).astype(F32)
    side = 2 * math.isqrt(count // 2)

    def quotient(value, by):
        return jnp.floor((value + 0.5) / by)

    lead = quotient(ids, side)
    strip = quotient(ids, count // 4)
    within = ids - strip * (count // 4)
    layer = quotient(within, count // 8)
    return (lead, ids - lead * side, within - layer * (count // 8), layer, strip)


def interior_points(shifts, table):
    side = math.isqrt(shifts.shape[-1] // 2)
    pos_x = RIM + (table[0] + shifts[0:1]) * ((1.0 - 2.0 * RIM) / side)
    pos_y = RIM + (table[1] + shifts[1:2]) * ((1.0 - 2.0 * RIM) / (2 * side))
    return pos_x, pos_y


def cycle_points(shifts, table):
    along = (table[2] + shifts[0:1]) / (shifts.shape[-1] // 8)
    depth = (table[3] + shifts[1:2]) * (0.5 * RIM)
    strip = table[4]
    pos_x = jnp.where(strip == 2.0, depth, jnp.where(strip == 3.0, 1.0 - depth, along))
    pos_y = jnp.where(strip == 0.0, depth, jnp.where(strip == 1.0, 1.0 - depth, along))
    return pos_x, pos_y


def column(row_value):
    size = row_value.shape[1]
    return jnp.broadcast_to(row_value, (size, size)).T


def wendland(first_x, first_y, second_x, second_y):
    gap_x = first_x - second_x
    gap_y = first_y - second_y
    radius = jnp.sqrt(gap_x * gap_x + gap_y * gap_y) / RIM
    inside = jnp.maximum(1.0 - radius, 0.0)
    return inside * inside * inside * inside * (4.0 * radius + 1.0)


def place():
    return lax.axis_index("bx"), lax.axis_index("by")


def send(source, target, send_sem, recv_sem, device):
    return pltpu.make_async_remote_copy(
        src_ref=source,
        dst_ref=target,
        send_sem=send_sem,
        recv_sem=recv_sem,
        device_id=device,
        device_id_type=pl.DeviceIdType.MESH,
    )


def front_kernel(
    jitter_far, noise_far, bases_far, near_basis, near_shift, factor, panel, schur,
    jitter, noise, basis_red_ref, sends, recvs, local,
):
    size = bases_far.shape[-1]
    mine = [
        pltpu.make_async_copy(jitter_far, jitter, local.at[0]),
        pltpu.make_async_copy(noise_far, noise, local.at[1]),
        pltpu.make_async_copy(bases_far.at[0], basis_red_ref, local.at[2]),
        pltpu.make_async_copy(bases_far.at[1], near_basis.at[1, 1], local.at[3]),
    ]
    for copy in mine:
        copy.start()
    index_x, index_y = place()
    last_x, last_y = lax.axis_size("bx") - 1, lax.axis_size("by") - 1
    have_x = {0: index_x > 0, 1: index_x >= 0, 2: index_x < last_x}
    have_y = {0: index_y > 0, 2: index_y < last_y}
    count = jnp.int32(0)
    barrier = pltpu.get_barrier_semaphore()
    for i in (0, 2):

        @pl.when(jnp.logical_not(have_x[i]))
        def _():
            near_basis[i] = jnp.zeros(near_basis.shape[1:], F32)
            near_shift[i] = jnp.zeros(near_shift.shape[1:], F32)

        @pl.when(jnp.logical_not(have_y[i]))
        def _():
            near_basis[:, i] = jnp.zeros((3,) + near_basis.shape[2:], F32)
            near_shift[:, i] = jnp.zeros((3,) + near_shift.shape[2:], F32)

    for i in (0, 2):

        @pl.when(have_x[i])
        def _():
            pl.semaphore_signal(barrier, inc=1, device_id=(index_x + i - 1, index_y), device_id_type=pl.DeviceIdType.MESH)

        @pl.when(have_y[i])
        def _():
            pl.semaphore_signal(barrier, inc=1, device_id=(index_x, index_y + i - 1), device_id_type=pl.DeviceIdType.MESH)

        count += have_x[i].astype(jnp.int32) + have_y[i].astype(jnp.int32)
    pl.semaphore_wait(barrier, count)
    for copy in mine:
        copy.wait()
    near_shift[1, 1] = jitter[:, size:]
    own = (near_basis.at[1, 1], near_shift.at[1, 1])
    near = (near_basis, near_shift)

    def along_x(i, part):
        return send(own[part], near[part].at[2 - i, 1], sends.at[0, i, 0, part], recvs.at[2 - i, 1, part], (index_x + i - 1, index_y))

    def along_y(i, k, part):
        source = own[part] if k == 1 else near[part].at[k, 1]
        return send(source, near[part].at[k, 2 - i], sends.at[1, i, k, part], recvs.at[k, 2 - i, part], (index_x, index_y + i - 1))

    def recv_wait(k, i, part):
        slot = near[part].at[k, i]
        send(slot, slot, sends.at[1, i, k, part], recvs.at[k, i, part], (index_x, index_y)).wait_recv()

    for i in (0, 2):

        @pl.when(have_x[i])
        def _():
            for part in (0, 1):
                along_x(i, part).start()

    for i in (0, 2):

        @pl.when(have_y[i])
        def _():
            for part in (0, 1):
                along_y(i, 1, part).start()

    table = point_table(size)
    shifts = jitter[...]
    inner_x, inner_y = interior_points(shifts[:, :size], table)
    cycle_x, cycle_y = cycle_points(shifts[:, size:], table)
    inner_cx, inner_cy = column(inner_x), column(inner_y)
    cycle_cx, cycle_cy = column(cycle_x), column(cycle_y)
    eye = identity(size)
    basis_red, basis_skel = basis_red_ref[...], near_basis[1, 1]
    red_t, skel_t = basis_red.T, basis_skel.T

    kern_inner = wendland(inner_cx, inner_cy, inner_x, inner_y) + eye * noise[:, :size]
    kern_mixed = wendland(inner_cx, inner_cy, cycle_x, cycle_y)
    kern_cycle = wendland(cycle_cx, cycle_cy, cycle_x, cycle_y) + eye * noise[:, size:]
    block = precise(red_t, precise(kern_inner, basis_red))
    mixed = precise(red_t, precise(kern_mixed, basis_skel))
    cycle = precise(skel_t, precise(kern_cycle, basis_skel))
    for k in (0, 2):

        @pl.when(have_x[k])
        def _():
            for part in (0, 1):
                recv_wait(k, 1, part)

        for i in (0, 2):

            @pl.when(have_x[k] & have_y[i])
            def _():
                for part in (0, 1):
                    along_y(i, k, part).start()

    lower, inverse = factor_block(block)
    rows = precise(inverse, mixed)
    factor[...] = lower
    panel[...] = rows
    schur[...] = cycle - precise(rows.T, rows)

    for i in (0, 2):
        for k in (0, 1, 2):

            @pl.when(have_x[k] & have_y[i])
            def _():
                for part in (0, 1):
                    recv_wait(k, i, part)
                    along_y(i, k, part).wait_send()

        @pl.when(have_x[i])
        def _():
            for part in (0, 1):
                along_x(i, part).wait_send()


def flip(index, mask, bit):
    return index + bit * (mask - 2 * mask * (index // mask % 2))


def family(index_x, index_y, p):
    to_x = flip(flip(index_x, 2, p // 8), 1, p // 2 % 2)
    to_y = flip(flip(index_y, 2, p // 4 % 2), 1, p % 2)
    return to_x, to_y


def enter(devices):
    barrier = pltpu.get_barrier_semaphore()
    for device in devices:
        pl.semaphore_signal(barrier, inc=1, device_id=device, device_id_type=pl.DeviceIdType.MESH)
    pl.semaphore_wait(barrier, len(devices))


def coupling_kernel(near_basis, near_shift, schur, couplings, pairs, near, diag, cross, sends, recvs):
    size = near_basis.shape[-1]
    shed = size - size // 4
    index_x, index_y = place()
    child_x, child_y = index_x % 2, index_y % 2
    own_slot = 2 * child_x + child_y
    other_slot = 2 * (1 - child_x) + child_y
    tile_slot = 4 * (2 * (index_x // 2 % 2) + index_y // 2 % 2) + own_slot
    boxes = {p: family(index_x, index_y, p) for p in range(1, 16)}
    enter(list(boxes.values()))
    across = send(schur, diag.at[own_slot], sends.at[0], recvs.at[0], boxes[2])
    beside = send(schur, diag.at[own_slot], sends.at[1], recvs.at[1], boxes[1])
    onward = send(diag.at[other_slot], diag.at[other_slot], sends.at[3], recvs.at[3], boxes[1])
    across.start()
    beside.start()
    diag[own_slot] = schur[...]
    table = point_table(size)
    cycle_x, cycle_y = cycle_points(near_shift[1, 1], table)
    column_x, column_y = column(cycle_x), column(cycle_y)
    skel_t = near_basis[1, 1].T

    def couple(n):
        step_x, step_y = OFFSETS[n]
        other_x, other_y = cycle_points(near_shift[1 + step_x, 1 + step_y], table)
        kern = wendland(column_x, column_y, step_x + other_x, step_y + other_y)
        block = precise(skel_t, precise(kern, near_basis[1 + step_x, 1 + step_y]))
        couplings[n] = block
        return block[shed:, shed:]

    tile = jnp.concatenate([couple(n) for n in range(4, 8)], axis=1)
    cross[...] = tile
    near[tile_slot] = tile
    for n in range(2):
        couple(n)
    tiles = [
        send(cross, near.at[tile_slot], sends.at[3 + p], recvs.at[3 + p], boxes[p])
        for p in range(15, 0, -1)
    ]
    for copy in tiles:
        copy.start()
    for n in range(2, 4):
        couple(n)
    across.wait_recv()
    onward.start()
    sources = []
    for slot in range(4):
        at = (1 + slot // 2 - child_x, 1 + slot % 2 - child_y)
        sources.append((near_basis[at],) + cycle_points(near_shift[at], table))
    count = 0
    for slot in range(3):
        basis_t = sources[slot][0].T
        from_x, from_y = column(sources[slot][1]), column(sources[slot][2])
        for other in range(slot + 1, 4):
            basis, to_x, to_y = sources[other]
            step_x, step_y = other // 2 - slot // 2, other % 2 - slot % 2
            kern = wendland(from_x, from_y, step_x + to_x, step_y + to_y)
            pairs[count] = precise(basis_t, precise(kern, basis))
            count += 1
    across.wait_send()
    for copy in [beside, onward] + tiles:
        copy.wait()


def gather_kernel(schur, diag, sends, recvs, local):
    size = schur.shape[0]
    half = size // 2
    index_x, index_y = place()
    side = index_y % 2
    parent = 2 * (index_x // 2 % 2) + index_y // 2 % 2
    beside = family(index_x, index_y, 1)
    afar = [family(index_x, index_y, p) for p in (12, 8, 4)]
    mine = pltpu.make_async_copy(schur, diag.at[parent], local.at[0])
    mine.start()
    enter([beside] + afar)
    rows = pl.ds(pl.multiple_of(side * half, 8), half)
    out = [
        send(schur.at[rows], diag.at[parent, rows], sends.at[p], recvs.at[p], device)
        for p, device in enumerate(afar)
    ]
    for copy in out:
        copy.start()
    onward = []
    for p in (2, 1, 0):
        other = (
            2 * ((index_x // 2 + (1, 1, 0)[p]) % 2) + (index_y // 2 + (1, 0, 1)[p]) % 2
        )
        out[p].wait_recv()
        block = diag.at[other, rows]
        onward.append(send(block, block, sends.at[3 + p], recvs.at[3 + p], beside))
        onward[-1].start()
    for copy in [mine] + onward:
        copy.wait()
    for copy in out:
        copy.wait_send()


def eliminate_large(shed_rows, kept_block, block, lower, panel_rows):
    size = shed_rows.shape[0]
    work = {
        i: shed_rows[i * block : (i + 1) * block, i * block :] for i in range(size // block)
    }
    for k in range(size // block):
        begin, end = k * block, (k + 1) * block
        factor, inverse = factor_block(work[k][:, :block])
        rest = precise(inverse, work[k][:, block:])
        lower[begin:end, begin:end] = factor
        rest_t = rest.T
        for i in range(k + 1, size // block):
            part_t = rest_t[(i - k - 1) * block : (i - k) * block]
            work[i] = work[i] - precise(part_t, rest[:, (i - k - 1) * block :])
            lower[i * block : (i + 1) * block, begin:end] = part_t
            lower[begin:end, i * block : (i + 1) * block] = jnp.zeros((block, block), F32)
        tail = rest[:, size - end :]
        panel_rows[begin:end] = tail
        kept_block = kept_block - precise(rest_t[size - end :], tail)
    return kept_block


def split_rows(grid, shed):
    top = jnp.concatenate(
        [
            jnp.concatenate([b[:shed, :shed] for b in row] + [b[:shed, shed:] for b in row], axis=1)
            for row in grid
        ],
        axis=0,
    )
    kept = jnp.concatenate(
        [jnp.concatenate([b[shed:, shed:] for b in row], axis=1) for row in grid], axis=0
    )
    return top, kept


def parent_kernel(
    diag, pairs, held_factor, held_panel, held_couplings,
    factor, panel, schur, box_factor, box_panel, couplings,
    lower, panel_rows, local,
):
    out = [
        pltpu.make_async_copy(held_factor, box_factor, local.at[0]),
        pltpu.make_async_copy(held_panel, box_panel, local.at[1]),
        pltpu.make_async_copy(held_couplings, couplings, local.at[2]),
    ]
    for copy in out:
        copy.start()
    size = pairs.shape[-1]
    shed = size - size // 4
    grid = [[None] * 4 for _ in range(4)]
    count = 0
    for slot in range(4):
        grid[slot][slot] = diag[slot]
        for other in range(slot + 1, 4):
            grid[slot][other] = pairs[count]
            grid[other][slot] = pairs[count].T
            count += 1
    rows, kept = split_rows(grid, shed)
    schur[...] = eliminate_large(rows, kept, size, lower, panel_rows)
    index_x, index_y = place()
    own = pl.ds(pl.multiple_of((2 * (index_x % 2) + index_y % 2) * shed, 8), shed)
    factor[...] = lower[own, :]
    panel[...] = panel_rows[own, :]
    for copy in out:
        copy.wait()


def grand_kernel(diag, near, factor, panel, schur, lower, panel_rows, kept_rows):
    size = diag.shape[-1]
    kept_size = size // 4
    shed = size - kept_size
    empty = jnp.zeros((kept_size, kept_size), F32)
    tiles = [near[g] for g in range(16)]
    turned = [tile.T for tile in tiles]

    def piece(e, c, f, d):
        gap_x = 2 * (f // 2 - e // 2) + d // 2 - c // 2
        gap_y = 2 * (f % 2 - e % 2) + d % 2 - c % 2
        if (gap_x, gap_y) in OFFSETS[4:]:
            at = OFFSETS[4:].index((gap_x, gap_y)) * kept_size
            return tiles[4 * e + c][:, at : at + kept_size]
        if (-gap_x, -gap_y) in OFFSETS[4:]:
            at = OFFSETS[4:].index((-gap_x, -gap_y)) * kept_size
            return turned[4 * f + d][at : at + kept_size]
        return empty

    grid = [[None] * 4 for _ in range(4)]
    for e in range(4):
        grid[e][e] = diag[e]
        for f in range(e + 1, 4):
            grid[e][f] = jnp.concatenate(
                [
                    jnp.concatenate([piece(e, c, f, d) for d in range(4)], axis=1)
                    for c in range(4)
                ],
                axis=0,
            )
            grid[f][e] = grid[e][f].T
    rows, kept = split_rows(grid, shed)
    kept_rows[...] = eliminate_large(rows, kept, size, lower, panel_rows)
    index_x, index_y = place()
    parent = 2 * (index_x // 2 % 2) + index_y // 2 % 2
    slot = 4 * parent + 2 * (index_x % 2) + index_y % 2

    def own(count):
        return pl.ds(pl.multiple_of(slot * count, 8), count)

    factor[...] = lower[own(shed // 4), :]
    panel[...] = panel_rows[own(shed // 4), :]
    schur[...] = kept_rows[own(size // 16), :]


def call(body, shapes, args, name, scratch=(), group=None, far=(), out_far=()):
    def spec(far_away):
        return pl.BlockSpec(memory_space=pltpu.HBM if far_away else pltpu.VMEM)

    return pl.pallas_call(
        body,
        out_shape=[jax.ShapeDtypeStruct(s, F32) for s in shapes],
        in_specs=[spec(i in far) for i in range(len(args))],
        out_specs=[spec(i in out_far) for i in range(len(shapes))],
        scratch_shapes=[
            pltpu.SemaphoreType.DMA(s[1:]) if s[0] == 0 else pltpu.VMEM(s, F32) for s in scratch
        ],
        compiler_params=pltpu.CompilerParams(
            vmem_limit_bytes=48 * 2**20,
            collective_id=group,
            has_side_effects=group is not None,
        ),
        name=name,
    )(*args)


def on_device(jitter, noise_var, bases):
    jitter, noise, bases = jitter[0, 0], noise_var[0], bases[0, 0]
    size = bases.shape[-1]
    kept = size // 4
    shed = size - kept
    square = (size, size)
    near_basis, near_shift, held_factor, held_panel, schur = call(
        front_kernel,
        [(3, 3) + square, (3, 3, 2, size)] + [square] * 3,
        (jitter, noise, bases),
        "front",
        [jitter.shape, noise.shape, square, (0, 2, 3, 3, 2), (0, 3, 3, 2), (0, 4)],
        group=0,
        far=(0, 1, 2),
    )
    held_couplings, pairs, near, quartet = call(
        coupling_kernel,
        [(8,) + square, (6,) + square, (16, kept, size), (4,) + square],
        (near_basis, near_shift, schur),
        "coupling",
        [(kept, size), (0, 19), (0, 19)],
        group=1,
    )
    wide = 4 * shed
    parent_factor, parent_panel, parent_schur, factor, panel, couplings = call(
        parent_kernel,
        [(shed, wide), (shed, size), square, square, square, (8,) + square],
        (quartet, pairs, held_factor, held_panel, held_couplings),
        "parent",
        [(wide, wide), (wide, size), (0, 3)],
        out_far=(3, 4, 5),
    )
    (upper,) = call(
        gather_kernel,
        [(4,) + square],
        (parent_schur,),
        "gather",
        [(0, 6), (0, 6), (0, 1)],
        group=2,
    )
    top_factor, top_panel, top_schur = call(
        grand_kernel,
        [(shed // 4, wide), (shed // 4, size), (size // 16, size)],
        (upper, near),
        "grand",
        [(wide, wide), (wide, size), square],
    )
    outs = (
        factor,
        panel,
        couplings,
        parent_factor,
        parent_panel,
        top_factor,
        top_panel,
        top_schur,
    )
    return tuple(value[None, None] for value in outs)


def solution(mesh):
    spec4 = P("bx", "by", None, None)
    spec5 = P("bx", "by", None, None, None)
    return jax.shard_map(
        on_device,
        mesh=mesh,
        in_specs=(spec4, P("bx", "by", None), spec5),
        out_specs=(spec4, spec4, spec5, spec4, spec4, spec4, spec4, spec4),
        check_vma=False,
    )
```

```python
import math

import jax
import jax.numpy as jnp
from jax import lax
from jax.experimental import pallas as pl
from jax.experimental.pallas import tpu as pltpu
from jax.sharding import PartitionSpec as P

RIM = 0.125
OFFSETS = ((-1, -1), (-1, 0), (-1, 1), (0, -1), (0, 1), (1, -1), (1, 0), (1, 1))
PANEL = 64
F32 = jnp.float32
BF16 = jnp.bfloat16


def pieces(value):
    high = value.astype(BF16)
    rest = value - high.astype(F32)
    middle = rest.astype(BF16)
    return high, middle, (rest - middle.astype(F32)).astype(BF16)


def joined(left, right, left_axis):
    lh, lm, ll = pieces(left)
    rh, rm, rl = pieces(right)
    lefts = jnp.concatenate([lh, lh, lm, lm, lh, ll], axis=left_axis)
    rights = jnp.concatenate([rh, rm, rh, rm, rl, rh], axis=0)
    return (lefts if left_axis else lefts.T), rights


def precise(left, right):
    lefts, rights = joined(left, right, 1)
    return jnp.dot(lefts, rights, preferred_element_type=F32)


def precise_t(left_t, right):
    lefts, rights = joined(left_t, right, 0)
    return jnp.dot(lefts, rights, preferred_element_type=F32)


def lane_copy(value, at):
    return jnp.take_along_axis(
        value, jnp.full(value.shape, at, jnp.int32), axis=1, mode="promise_in_bounds"
    )


def factor_block(block, panel=PANEL):
    size = block.shape[0]
    rows = [block[8 * i : 8 * i + 8] for i in range(size // 8)]
    sub = lax.broadcasted_iota(jnp.int32, rows[0].shape, 0)
    lane = lax.broadcasted_iota(jnp.int32, rows[0].shape, 1)
    uppers, diags = [], []
    for start in range(0, size, panel):
        stop = min(start + panel, size)
        first, last = start // 8, stop // 8
        for g in range(first, last):
            span = range(g, last)
            cols = {(m, i): lane_copy(rows[i], 8 * g + m) for i in span for m in range(8)}
            here = (lane >= 8 * g) & (lane < 8 * g + 8)
            unit = jnp.where(sub == lane - 8 * g, 1.0, 0.0)
            for i in span:
                rows[i] = jnp.where(here, unit if i == g else 0.0, rows[i])
            diag = jnp.zeros_like(rows[g])
            for j in range(8):

                def row(value):
                    return jnp.broadcast_to(value[j : j + 1], value.shape)

                inv = lax.rsqrt(row(cols[j, g]))
                u_c = {m: row(cols[m, g]) * inv for m in range(j + 1, 8)}
                mults = {}
                for i in span:
                    mults[i] = cols[j, i] * inv
                    for m in range(j + 1, 8):
                        cols[m, i] = cols[m, i] - mults[i] * u_c[m]
                u = row(rows[g]) * inv
                diag = jnp.where((lane == 8 * g + j) & (sub >= j), mults[g], diag)
                below = jnp.where(sub > j, mults[g], 0.0)
                rows[g] = jnp.where(sub == j, u, rows[g] - below * u)
                for i in span[1:]:
                    rows[i] = rows[i] - mults[i] * u
            diags.append(diag)
            uppers.append(jnp.where(lane >= 8 * g + 8, rows[g], 0.0))
        if stop < size:
            kept = [
                jnp.where((lane >= 8 * g + 8) & (lane < stop), 0.0, rows[g])
                for g in range(first, last)
            ]
            change = precise_t(
                jnp.concatenate(uppers[first:last], axis=0), jnp.concatenate(kept, axis=0)
            )
            gone = (lane >= start) & (lane < stop)
            for i in range(last, size // 8):
                rows[i] = jnp.where(gone, 0.0, rows[i]) - change[8 * i : 8 * i + 8]
    lower = jnp.concatenate(uppers, axis=0).T + jnp.concatenate(diags, axis=0)
    full = jnp.concatenate(rows, axis=0)
    row_id = lax.broadcasted_iota(jnp.int32, full.shape, 0)
    col_id = lax.broadcasted_iota(jnp.int32, full.shape, 1)
    return lower, jnp.where(col_id < row_id // 8 * 8 + 8, full, 0.0)


def identity(size):
    row_id = lax.broadcasted_iota(jnp.int32, (size, size), 0)
    col_id = lax.broadcasted_iota(jnp.int32, (size, size), 1)
    return jnp.where(row_id == col_id, 1.0, 0.0).astype(F32)


def point_table(count):
    ids = lax.broadcasted_iota(jnp.int32, (1, count), 1).astype(F32)
    side = 2 * math.isqrt(count // 2)

    def quotient(value, by):
        return jnp.floor((value + 0.5) / by)

    lead = quotient(ids, side)
    strip = quotient(ids, count // 4)
    within = ids - strip * (count // 4)
    layer = quotient(within, count // 8)
    return (lead, ids - lead * side, within - layer * (count // 8), layer, strip)


def interior_points(shifts, table):
    side = math.isqrt(shifts.shape[-1] // 2)
    pos_x = RIM + (table[0] + shifts[0:1]) * ((1.0 - 2.0 * RIM) / side)
    pos_y = RIM + (table[1] + shifts[1:2]) * ((1.0 - 2.0 * RIM) / (2 * side))
    return pos_x, pos_y


def cycle_points(shifts, table):
    along = (table[2] + shifts[0:1]) / (shifts.shape[-1] // 8)
    depth = (table[3] + shifts[1:2]) * (0.5 * RIM)
    strip = table[4]
    pos_x = jnp.where(strip == 2.0, depth, jnp.where(strip == 3.0, 1.0 - depth, along))
    pos_y = jnp.where(strip == 0.0, depth, jnp.where(strip == 1.0, 1.0 - depth, along))
    return pos_x, pos_y


def column(row_value):
    size = row_value.shape[1]
    return jnp.broadcast_to(row_value, (size, size)).T


def wendland(first_x, first_y, second_x, second_y):
    gap_x = first_x - second_x
    gap_y = first_y - second_y
    radius = jnp.sqrt(gap_x * gap_x + gap_y * gap_y) / RIM
    inside = jnp.maximum(1.0 - radius, 0.0)
    return inside * inside * inside * inside * (4.0 * radius + 1.0)


def place():
    return lax.axis_index("bx"), lax.axis_index("by")


def send(source, target, send_sem, recv_sem, device):
    return pltpu.make_async_remote_copy(
        src_ref=source,
        dst_ref=target,
        send_sem=send_sem,
        recv_sem=recv_sem,
        device_id=device,
        device_id_type=pl.DeviceIdType.MESH,
    )


def facing(step_x, step_y):
    high_x, high_y = int(step_x > 0), int(step_y > 0)
    if step_y == 0:
        return ((4 + 2 * high_x, 2, None), (0, 4, high_x))
    if step_x == 0:
        return ((2 * high_y, 2, None), (4, 4, high_y))
    return ((2 * high_y, 2, high_x), (4 + 2 * high_x, 2, high_y))


def some_rows(ref, part):
    first, count, half = part
    return ref.at[pl.ds(first, count)] if half is None else ref.at[pl.ds(first, count), half]


def front_kernel(
    jitter_far, noise_far, bases_far, near_basis, near_shift, factor, panel, schur,
    jitter, noise, basis_red_ref, sends, recvs, local,
):
    size = bases_far.shape[-1]
    mine = [
        pltpu.make_async_copy(jitter_far, jitter, local.at[0]),
        pltpu.make_async_copy(noise_far, noise, local.at[1]),
        pltpu.make_async_copy(bases_far.at[0], basis_red_ref, local.at[2]),
        pltpu.make_async_copy(bases_far.at[1], near_basis.at[1, 1], local.at[3]),
    ]
    for copy in mine:
        copy.start()
    index_x, index_y = place()
    last_x, last_y = lax.axis_size("bx") - 1, lax.axis_size("by") - 1
    have_x = {-1: index_x > 0, 0: index_x >= 0, 1: index_x < last_x}
    have_y = {-1: index_y > 0, 0: index_y >= 0, 1: index_y < last_y}
    have = [have_x[o[0]] & have_y[o[1]] for o in OFFSETS]
    whole = []
    for step_x, step_y in OFFSETS:
        if step_y == 0:
            whole.append(index_x % 2 == int(step_x < 0))
        elif step_x == 0:
            whole.append(index_y % 2 == int(step_y < 0))
        else:
            whole.append(None)
    for step_x, step_y in OFFSETS:
        near_basis[1 + step_x, 1 + step_y] = jnp.zeros(near_basis.shape[2:], F32)
        near_shift[1 + step_x, 1 + step_y] = jnp.zeros(near_shift.shape[2:], F32)
    barrier = pltpu.get_barrier_semaphore()
    count = jnp.int32(0)
    for n, (step_x, step_y) in enumerate(OFFSETS):

        @pl.when(have[n])
        def _():
            pl.semaphore_signal(
                barrier,
                inc=1,
                device_id=(index_x + step_x, index_y + step_y),
                device_id_type=pl.DeviceIdType.MESH,
            )

        count += have[n].astype(jnp.int32)
    for copy in mine:
        copy.wait()
    near_shift[1, 1] = jitter[:, size:]
    pl.semaphore_wait(barrier, count)

    def out(n, kind):
        step_x, step_y = OFFSETS[n]
        there = OFFSETS.index((-step_x, -step_y))
        device = (index_x + step_x, index_y + step_y)
        own, slot = near_basis.at[1, 1], near_basis.at[1 - step_x, 1 - step_y]
        if kind == 3:
            own, slot = near_shift.at[1, 1], near_shift.at[1 - step_x, 1 - step_y]
        elif kind:
            part = facing(step_x, step_y)[kind - 1]
            own, slot = some_rows(own, part), some_rows(slot, part)
        return send(own, slot, sends.at[n, kind], recvs.at[there, kind], device)

    def come(n, kind):
        step_x, step_y = OFFSETS[n]
        slot = near_basis.at[1 + step_x, 1 + step_y]
        if kind == 3:
            slot = near_shift.at[1 + step_x, 1 + step_y]
        elif kind:
            slot = some_rows(slot, facing(-step_x, -step_y)[kind - 1])
        device = (index_x + step_x, index_y + step_y)
        return send(slot, slot, sends.at[n, kind], recvs.at[n, kind], device)

    def each(n, act):
        if whole[n] is None:

            @pl.when(have[n])
            def _():
                for kind in (3, 1, 2):
                    act(n, kind)

        else:

            @pl.when(have[n] & whole[n])
            def _():
                for kind in (3, 0):
                    act(n, kind)

            @pl.when(have[n] & jnp.logical_not(whole[n]))
            def _():
                for kind in (3, 1, 2):
                    act(n, kind)

    for n in (1, 6, 3, 4, 0, 2, 5, 7):
        each(n, lambda n, kind: out(n, kind).start())
    table = point_table(size)
    shifts = jitter[...]
    inner_x, inner_y = interior_points(shifts[:, :size], table)
    cycle_x, cycle_y = cycle_points(shifts[:, size:], table)
    inner_cx, inner_cy = column(inner_x), column(inner_y)
    cycle_cx, cycle_cy = column(cycle_x), column(cycle_y)
    eye = identity(size)
    square = (size, size)
    basis_red = basis_red_ref[...].reshape(square)
    basis_skel = near_basis[1, 1].reshape(square)
    red_t, skel_t = basis_red.T, basis_skel.T

    kern_inner = wendland(inner_cx, inner_cy, inner_x, inner_y) + eye * noise[:, :size]
    kern_mixed = wendland(inner_cx, inner_cy, cycle_x, cycle_y)
    kern_cycle = wendland(cycle_cx, cycle_cy, cycle_x, cycle_y) + eye * noise[:, size:]
    block = precise(red_t, precise(kern_inner, basis_red))
    mixed = precise(red_t, precise(kern_mixed, basis_skel))
    cycle = precise(skel_t, precise(kern_cycle, basis_skel))
    lower, inverse = factor_block(block)
    rows = precise(inverse, mixed)
    factor[...] = lower
    panel[...] = rows
    schur[...] = cycle - precise(rows.T, rows)

    def finish(n, kind):
        come(n, kind).wait_recv()
        out(n, kind).wait_send()

    for n in range(8):
        each(n, finish)


def flip(index, mask, bit):
    return index + bit * (mask - 2 * mask * (index // mask % 2))


def family(index_x, index_y, p):
    to_x = flip(flip(index_x, 2, p // 8), 1, p // 2 % 2)
    to_y = flip(flip(index_y, 2, p // 4 % 2), 1, p % 2)
    return to_x, to_y


def enter(devices):
    barrier = pltpu.get_barrier_semaphore()
    for device in devices:
        pl.semaphore_signal(barrier, inc=1, device_id=device, device_id_type=pl.DeviceIdType.MESH)
    pl.semaphore_wait(barrier, len(devices))


def coupling_kernel(near_basis, near_shift, schur, couplings, pairs, near, diag, cross, kin, sends, recvs):
    size = near_basis.shape[-1]
    shed = size - size // 4
    index_x, index_y = place()
    child_x, child_y = index_x % 2, index_y % 2
    own_slot = 2 * child_x + child_y
    other_slot = 2 * (1 - child_x) + child_y
    tile_slot = 4 * (2 * (index_x // 2 % 2) + index_y // 2 % 2) + own_slot
    boxes = {p: family(index_x, index_y, p) for p in range(1, 16)}
    enter(list(boxes.values()))
    across = send(schur, diag.at[own_slot], sends.at[0], recvs.at[0], boxes[2])
    beside = send(schur, diag.at[own_slot], sends.at[1], recvs.at[1], boxes[1])
    onward = send(diag.at[other_slot], diag.at[other_slot], sends.at[3], recvs.at[3], boxes[1])
    across_at = (2 - 2 * child_x, 1)
    beside_at = (1, 2 - 2 * child_y)
    relay = send(near_basis.at[across_at], kin.at[other_slot], sends.at[2], recvs.at[2], boxes[1])
    across.start()
    beside.start()
    relay.start()
    kin[own_slot] = near_basis[1, 1]
    kin[2 * (1 - child_x) + child_y] = near_basis[across_at]
    kin[2 * child_x + 1 - child_y] = near_basis[beside_at]
    diag[own_slot] = schur[...]
    table = point_table(size)
    cycle_x, cycle_y = cycle_points(near_shift[1, 1], table)
    column_x, column_y = column(cycle_x), column(cycle_y)
    skel_t = near_basis[1, 1].T

    def couple(n):
        step_x, step_y = OFFSETS[n]
        other_x, other_y = cycle_points(near_shift[1 + step_x, 1 + step_y], table)
        kern = wendland(column_x, column_y, step_x + other_x, step_y + other_y)
        block = precise(skel_t, precise(kern, near_basis[1 + step_x, 1 + step_y]))
        couplings[n] = block
        return block[shed:, shed:]

    tile = jnp.concatenate([couple(n) for n in range(4, 8)], axis=1)
    cross[...] = tile
    near[tile_slot] = tile
    for n in range(2):
        couple(n)
    tiles = [
        send(cross, near.at[tile_slot], sends.at[3 + p], recvs.at[3 + p], boxes[p])
        for p in range(15, 0, -1)
    ]
    for copy in tiles:
        copy.start()
    for n in range(2, 4):
        couple(n)
    across.wait_recv()
    onward.start()
    relay.wait()
    sources = []
    for slot in range(4):
        at = (1 + slot // 2 - child_x, 1 + slot % 2 - child_y)
        sources.append((kin[slot],) + cycle_points(near_shift[at], table))
    count = 0
    for slot in range(3):
        basis_t = sources[slot][0].T
        from_x, from_y = column(sources[slot][1]), column(sources[slot][2])
        for other in range(slot + 1, 4):
            basis, to_x, to_y = sources[other]
            step_x, step_y = other // 2 - slot // 2, other % 2 - slot % 2
            kern = wendland(from_x, from_y, step_x + to_x, step_y + to_y)
            pairs[count] = precise(basis_t, precise(kern, basis))
            count += 1
    across.wait_send()
    for copy in [beside, onward] + tiles:
        copy.wait()


def gather_kernel(schur, diag, sends, recvs, local):
    size = schur.shape[0]
    half = size // 2
    index_x, index_y = place()
    side = index_y % 2
    parent = 2 * (index_x // 2 % 2) + index_y // 2 % 2
    beside = family(index_x, index_y, 1)
    afar = [family(index_x, index_y, p) for p in (12, 8, 4)]
    mine = pltpu.make_async_copy(schur, diag.at[parent], local.at[0])
    mine.start()
    enter([beside] + afar)
    rows = pl.ds(pl.multiple_of(side * half, 8), half)
    out = [
        send(schur.at[rows], diag.at[parent, rows], sends.at[p], recvs.at[p], device)
        for p, device in enumerate(afar)
    ]
    for copy in out:
        copy.start()
    onward = []
    for p in (2, 1, 0):
        other = (
            2 * ((index_x // 2 + (1, 1, 0)[p]) % 2) + (index_y // 2 + (1, 0, 1)[p]) % 2
        )
        out[p].wait_recv()
        block = diag.at[other, rows]
        onward.append(send(block, block, sends.at[3 + p], recvs.at[3 + p], beside))
        onward[-1].start()
    for copy in [mine] + onward:
        copy.wait()
    for copy in out:
        copy.wait_send()


def eliminate_large(shed_rows, kept_block, block, lower, panel_rows):
    size = shed_rows.shape[0]
    work = {
        i: shed_rows[i * block : (i + 1) * block, i * block :] for i in range(size // block)
    }
    for k in range(size // block):
        begin, end = k * block, (k + 1) * block
        factor, inverse = factor_block(work[k][:, :block])
        rest = precise(inverse, work[k][:, block:])
        lower[begin:end, begin:end] = factor
        rest_t = rest.T
        for i in range(k + 1, size // block):
            part_t = rest_t[(i - k - 1) * block : (i - k) * block]
            work[i] = work[i] - precise(part_t, rest[:, (i - k - 1) * block :])
            lower[i * block : (i + 1) * block, begin:end] = part_t
            lower[begin:end, i * block : (i + 1) * block] = jnp.zeros((block, block), F32)
        tail = rest[:, size - end :]
        panel_rows[begin:end] = tail
        kept_block = kept_block - precise(rest_t[size - end :], tail)
    return kept_block


def split_rows(grid, shed):
    top = jnp.concatenate(
        [
            jnp.concatenate([b[:shed, :shed] for b in row] + [b[:shed, shed:] for b in row], axis=1)
            for row in grid
        ],
        axis=0,
    )
    kept = jnp.concatenate(
        [jnp.concatenate([b[shed:, shed:] for b in row], axis=1) for row in grid], axis=0
    )
    return top, kept


def parent_kernel(
    diag, pairs, held_factor, held_panel, held_couplings,
    factor, panel, schur, box_factor, box_panel, couplings,
    lower, panel_rows, local,
):
    out = [
        pltpu.make_async_copy(held_factor, box_factor, local.at[0]),
        pltpu.make_async_copy(held_panel, box_panel, local.at[1]),
        pltpu.make_async_copy(held_couplings, couplings, local.at[2]),
    ]
    for copy in out:
        copy.start()
    size = pairs.shape[-1]
    shed = size - size // 4
    grid = [[None] * 4 for _ in range(4)]
    count = 0
    for slot in range(4):
        grid[slot][slot] = diag[slot]
        for other in range(slot + 1, 4):
            grid[slot][other] = pairs[count]
            grid[other][slot] = pairs[count].T
            count += 1
    rows, kept = split_rows(grid, shed)
    schur[...] = eliminate_large(rows, kept, size, lower, panel_rows)
    index_x, index_y = place()
    own = pl.ds(pl.multiple_of((2 * (index_x % 2) + index_y % 2) * shed, 8), shed)
    factor[...] = lower[own, :]
    panel[...] = panel_rows[own, :]
    for copy in out:
        copy.wait()


def grand_kernel(diag, near, factor, panel, schur, lower, panel_rows, kept_rows):
    size = diag.shape[-1]
    kept_size = size // 4
    shed = size - kept_size
    empty = jnp.zeros((kept_size, kept_size), F32)
    tiles = [near[g] for g in range(16)]
    turned = [tile.T for tile in tiles]

    def piece(e, c, f, d):
        gap_x = 2 * (f // 2 - e // 2) + d // 2 - c // 2
        gap_y = 2 * (f % 2 - e % 2) + d % 2 - c % 2
        if (gap_x, gap_y) in OFFSETS[4:]:
            at = OFFSETS[4:].index((gap_x, gap_y)) * kept_size
            return tiles[4 * e + c][:, at : at + kept_size]
        if (-gap_x, -gap_y) in OFFSETS[4:]:
            at = OFFSETS[4:].index((-gap_x, -gap_y)) * kept_size
            return turned[4 * f + d][at : at + kept_size]
        return empty

    grid = [[None] * 4 for _ in range(4)]
    for e in range(4):
        grid[e][e] = diag[e]
        for f in range(e + 1, 4):
            grid[e][f] = jnp.concatenate(
                [
                    jnp.concatenate([piece(e, c, f, d) for d in range(4)], axis=1)
                    for c in range(4)
                ],
                axis=0,
            )
            grid[f][e] = grid[e][f].T
    rows, kept = split_rows(grid, shed)
    kept_rows[...] = eliminate_large(rows, kept, size, lower, panel_rows)
    index_x, index_y = place()
    parent = 2 * (index_x // 2 % 2) + index_y // 2 % 2
    slot = 4 * parent + 2 * (index_x % 2) + index_y % 2

    def own(count):
        return pl.ds(pl.multiple_of(slot * count, 8), count)

    factor[...] = lower[own(shed // 4), :]
    panel[...] = panel_rows[own(shed // 4), :]
    schur[...] = kept_rows[own(size // 16), :]


def call(body, shapes, args, name, scratch=(), group=None, far=(), out_far=()):
    def spec(far_away):
        return pl.BlockSpec(memory_space=pltpu.HBM if far_away else pltpu.VMEM)

    return pl.pallas_call(
        body,
        out_shape=[jax.ShapeDtypeStruct(s, F32) for s in shapes],
        in_specs=[spec(i in far) for i in range(len(args))],
        out_specs=[spec(i in out_far) for i in range(len(shapes))],
        scratch_shapes=[
            pltpu.SemaphoreType.DMA(s[1:]) if s[0] == 0 else pltpu.VMEM(s, F32) for s in scratch
        ],
        compiler_params=pltpu.CompilerParams(
            vmem_limit_bytes=48 * 2**20,
            collective_id=group,
            has_side_effects=group is not None,
        ),
        name=name,
    )(*args)


def on_device(jitter, noise_var, bases):
    jitter, noise, bases = jitter[0, 0], noise_var[0], bases[0, 0]
    size = bases.shape[-1]
    kept = size // 4
    shed = size - kept
    square = (size, size)
    strips = (8, 2, size // 16, size)
    near_basis, near_shift, held_factor, held_panel, schur = call(
        front_kernel,
        [(3, 3) + strips, (3, 3, 2, size)] + [square] * 3,
        (jitter, noise, bases.reshape((2,) + strips)),
        "front",
        [jitter.shape, noise.shape, strips, (0, 8, 4), (0, 8, 4), (0, 4)],
        group=0,
        far=(0, 1, 2),
    )
    held_couplings, pairs, near, quartet = call(
        coupling_kernel,
        [(8,) + square, (6,) + square, (16, kept, size), (4,) + square],
        (near_basis.reshape((3, 3) + square), near_shift, schur),
        "coupling",
        [(kept, size), (4,) + square, (0, 19), (0, 19)],
        group=1,
    )
    wide = 4 * shed
    parent_factor, parent_panel, parent_schur, factor, panel, couplings = call(
        parent_kernel,
        [(shed, wide), (shed, size), square, square, square, (8,) + square],
        (quartet, pairs, held_factor, held_panel, held_couplings),
        "parent",
        [(wide, wide), (wide, size), (0, 3)],
        out_far=(3, 4, 5),
    )
    (upper,) = call(
        gather_kernel,
        [(4,) + square],
        (parent_schur,),
        "gather",
        [(0, 6), (0, 6), (0, 1)],
        group=2,
    )
    top_factor, top_panel, top_schur = call(
        grand_kernel,
        [(shed // 4, wide), (shed // 4, size), (size // 16, size)],
        (upper, near),
        "grand",
        [(wide, wide), (wide, size), square],
    )
    outs = (
        factor,
        panel,
        couplings,
        parent_factor,
        parent_panel,
        top_factor,
        top_panel,
        top_schur,
    )
    return tuple(value[None, None] for value in outs)


def solution(mesh):
    spec4 = P("bx", "by", None, None)
    spec5 = P("bx", "by", None, None, None)
    return jax.shard_map(
        on_device,
        mesh=mesh,
        in_specs=(spec4, P("bx", "by", None), spec5),
        out_specs=(spec4, spec4, spec5, spec4, spec4, spec4, spec4, spec4),
        check_vma=False,
    )
```

```python
import math

import jax
import jax.numpy as jnp
from jax import lax
from jax.experimental import pallas as pl
from jax.experimental.pallas import tpu as pltpu
from jax.sharding import PartitionSpec as P

RIM = 0.125
OFFSETS = ((-1, -1), (-1, 0), (-1, 1), (0, -1), (0, 1), (1, -1), (1, 0), (1, 1))
PANEL = 64
F32 = jnp.float32
BF16 = jnp.bfloat16


def pieces(value):
    high = value.astype(BF16)
    rest = value - high.astype(F32)
    middle = rest.astype(BF16)
    return high, middle, (rest - middle.astype(F32)).astype(BF16)


def joined(left, right, left_axis):
    lh, lm, ll = pieces(left)
    rh, rm, rl = pieces(right)
    lefts = jnp.concatenate([lh, lh, lm, lm, lh, ll], axis=left_axis)
    rights = jnp.concatenate([rh, rm, rh, rm, rl, rh], axis=0)
    return (lefts if left_axis else lefts.T), rights


def precise(left, right):
    lefts, rights = joined(left, right, 1)
    return jnp.dot(lefts, rights, preferred_element_type=F32)


def precise_t(left_t, right):
    lefts, rights = joined(left_t, right, 0)
    return jnp.dot(lefts, rights, preferred_element_type=F32)


def lane_copy(value, at):
    return jnp.take_along_axis(
        value, jnp.full(value.shape, at, jnp.int32), axis=1, mode="promise_in_bounds"
    )


def factor_block(block, panel=PANEL):
    size = block.shape[0]
    rows = [block[8 * i : 8 * i + 8] for i in range(size // 8)]
    sub = lax.broadcasted_iota(jnp.int32, rows[0].shape, 0)
    lane = lax.broadcasted_iota(jnp.int32, rows[0].shape, 1)
    uppers, diags = [], []
    for start in range(0, size, panel):
        stop = min(start + panel, size)
        first, last = start // 8, stop // 8
        for g in range(first, last):
            span = range(g, last)
            cols = {(m, i): lane_copy(rows[i], 8 * g + m) for i in span for m in range(8)}
            here = (lane >= 8 * g) & (lane < 8 * g + 8)
            unit = jnp.where(sub == lane - 8 * g, 1.0, 0.0)
            for i in span:
                rows[i] = jnp.where(here, unit if i == g else 0.0, rows[i])
            diag = jnp.zeros_like(rows[g])
            for j in range(8):

                def row(value):
                    return jnp.broadcast_to(value[j : j + 1], value.shape)

                inv = lax.rsqrt(row(cols[j, g]))
                u_c = {m: row(cols[m, g]) * inv for m in range(j + 1, 8)}
                mults = {}
                for i in span:
                    mults[i] = cols[j, i] * inv
                    for m in range(j + 1, 8):
                        cols[m, i] = cols[m, i] - mults[i] * u_c[m]
                u = row(rows[g]) * inv
                diag = jnp.where((lane == 8 * g + j) & (sub >= j), mults[g], diag)
                below = jnp.where(sub > j, mults[g], 0.0)
                rows[g] = jnp.where(sub == j, u, rows[g] - below * u)
                for i in span[1:]:
                    rows[i] = rows[i] - mults[i] * u
            diags.append(diag)
            uppers.append(jnp.where(lane >= 8 * g + 8, rows[g], 0.0))
        if stop < size:
            kept = [
                jnp.where((lane >= 8 * g + 8) & (lane < stop), 0.0, rows[g])
                for g in range(first, last)
            ]
            change = precise_t(
                jnp.concatenate(uppers[first:last], axis=0), jnp.concatenate(kept, axis=0)
            )
            gone = (lane >= start) & (lane < stop)
            for i in range(last, size // 8):
                rows[i] = jnp.where(gone, 0.0, rows[i]) - change[8 * i : 8 * i + 8]
    lower = jnp.concatenate(uppers, axis=0).T + jnp.concatenate(diags, axis=0)
    full = jnp.concatenate(rows, axis=0)
    row_id = lax.broadcasted_iota(jnp.int32, full.shape, 0)
    col_id = lax.broadcasted_iota(jnp.int32, full.shape, 1)
    return lower, jnp.where(col_id < row_id // 8 * 8 + 8, full, 0.0)


def identity(size):
    row_id = lax.broadcasted_iota(jnp.int32, (size, size), 0)
    col_id = lax.broadcasted_iota(jnp.int32, (size, size), 1)
    return jnp.where(row_id == col_id, 1.0, 0.0).astype(F32)


def point_table(count):
    ids = lax.broadcasted_iota(jnp.int32, (1, count), 1).astype(F32)
    side = 2 * math.isqrt(count // 2)

    def quotient(value, by):
        return jnp.floor((value + 0.5) / by)

    lead = quotient(ids, side)
    strip = quotient(ids, count // 4)
    within = ids - strip * (count // 4)
    layer = quotient(within, count // 8)
    return (lead, ids - lead * side, within - layer * (count // 8), layer, strip)


def interior_points(shifts, table):
    side = math.isqrt(shifts.shape[-1] // 2)
    pos_x = RIM + (table[0] + shifts[0:1]) * ((1.0 - 2.0 * RIM) / side)
    pos_y = RIM + (table[1] + shifts[1:2]) * ((1.0 - 2.0 * RIM) / (2 * side))
    return pos_x, pos_y


def cycle_points(shifts, table):
    along = (table[2] + shifts[0:1]) / (shifts.shape[-1] // 8)
    depth = (table[3] + shifts[1:2]) * (0.5 * RIM)
    strip = table[4]
    pos_x = jnp.where(strip == 2.0, depth, jnp.where(strip == 3.0, 1.0 - depth, along))
    pos_y = jnp.where(strip == 0.0, depth, jnp.where(strip == 1.0, 1.0 - depth, along))
    return pos_x, pos_y


def column(row_value):
    size = row_value.shape[1]
    return jnp.broadcast_to(row_value, (size, size)).T


def wendland(first_x, first_y, second_x, second_y):
    gap_x = first_x - second_x
    gap_y = first_y - second_y
    radius = jnp.sqrt(gap_x * gap_x + gap_y * gap_y) / RIM
    inside = jnp.maximum(1.0 - radius, 0.0)
    return inside * inside * inside * inside * (4.0 * radius + 1.0)


def place():
    return lax.axis_index("bx"), lax.axis_index("by")


def send(source, target, send_sem, recv_sem, device):
    return pltpu.make_async_remote_copy(
        src_ref=source,
        dst_ref=target,
        send_sem=send_sem,
        recv_sem=recv_sem,
        device_id=device,
        device_id_type=pl.DeviceIdType.MESH,
    )


def facing(step_x, step_y):
    high_x, high_y = int(step_x > 0), int(step_y > 0)
    if step_y == 0:
        return ((4 + 2 * high_x, 2, None), (0, 4, high_x))
    if step_x == 0:
        return ((2 * high_y, 2, None), (4, 4, high_y))
    return ((2 * high_y, 2, high_x), (4 + 2 * high_x, 2, high_y))


def some_rows(ref, part):
    first, count, half = part
    return ref.at[pl.ds(first, count)] if half is None else ref.at[pl.ds(first, count), half]


def front_kernel(
    jitter_far, noise_far, bases_far, near_basis, near_shift, factor, panel, schur,
    jitter, noise, basis_red_ref, sends, recvs, local,
):
    size = bases_far.shape[-1]
    mine = [
        pltpu.make_async_copy(jitter_far, jitter, local.at[0]),
        pltpu.make_async_copy(noise_far, noise, local.at[1]),
        pltpu.make_async_copy(bases_far.at[0], basis_red_ref, local.at[2]),
        pltpu.make_async_copy(bases_far.at[1], near_basis.at[1, 1], local.at[3]),
    ]
    for copy in mine:
        copy.start()
    index_x, index_y = place()
    last_x, last_y = lax.axis_size("bx") - 1, lax.axis_size("by") - 1
    have_x = {-1: index_x > 0, 0: index_x >= 0, 1: index_x < last_x}
    have_y = {-1: index_y > 0, 0: index_y >= 0, 1: index_y < last_y}
    have = [have_x[o[0]] & have_y[o[1]] for o in OFFSETS]
    whole = []
    for step_x, step_y in OFFSETS:
        if step_y == 0:
            whole.append(index_x % 2 == int(step_x < 0))
        elif step_x == 0:
            whole.append(index_y % 2 == int(step_y < 0))
        else:
            whole.append(None)
    for step_x, step_y in OFFSETS:
        near_basis[1 + step_x, 1 + step_y] = jnp.zeros(near_basis.shape[2:], F32)
        near_shift[1 + step_x, 1 + step_y] = jnp.zeros(near_shift.shape[2:], F32)
    barrier = pltpu.get_barrier_semaphore()
    count = jnp.int32(0)
    for n, (step_x, step_y) in enumerate(OFFSETS):

        @pl.when(have[n])
        def _():
            pl.semaphore_signal(
                barrier,
                inc=1,
                device_id=(index_x + step_x, index_y + step_y),
                device_id_type=pl.DeviceIdType.MESH,
            )

        count += have[n].astype(jnp.int32)
    for copy in mine:
        copy.wait()
    near_shift[1, 1] = jitter[:, size:]
    pl.semaphore_wait(barrier, count)

    def out(n, kind):
        step_x, step_y = OFFSETS[n]
        there = OFFSETS.index((-step_x, -step_y))
        device = (index_x + step_x, index_y + step_y)
        own, slot = near_basis.at[1, 1], near_basis.at[1 - step_x, 1 - step_y]
        if kind == 3:
            own, slot = near_shift.at[1, 1], near_shift.at[1 - step_x, 1 - step_y]
        elif kind:
            part = facing(step_x, step_y)[kind - 1]
            own, slot = some_rows(own, part), some_rows(slot, part)
        return send(own, slot, sends.at[n, kind], recvs.at[there, kind], device)

    def come(n, kind):
        step_x, step_y = OFFSETS[n]
        slot = near_basis.at[1 + step_x, 1 + step_y]
        if kind == 3:
            slot = near_shift.at[1 + step_x, 1 + step_y]
        elif kind:
            slot = some_rows(slot, facing(-step_x, -step_y)[kind - 1])
        device = (index_x + step_x, index_y + step_y)
        return send(slot, slot, sends.at[n, kind], recvs.at[n, kind], device)

    def each(n, act):
        if whole[n] is None:

            @pl.when(have[n])
            def _():
                for kind in (3, 1, 2):
                    act(n, kind)

        else:

            @pl.when(have[n] & whole[n])
            def _():
                for kind in (3, 0):
                    act(n, kind)

            @pl.when(have[n] & jnp.logical_not(whole[n]))
            def _():
                for kind in (3, 1, 2):
                    act(n, kind)

    for n in (1, 6, 3, 4, 0, 2, 5, 7):
        each(n, lambda n, kind: out(n, kind).start())
    table = point_table(size)
    shifts = jitter[...]
    inner_x, inner_y = interior_points(shifts[:, :size], table)
    cycle_x, cycle_y = cycle_points(shifts[:, size:], table)
    inner_cx, inner_cy = column(inner_x), column(inner_y)
    cycle_cx, cycle_cy = column(cycle_x), column(cycle_y)
    eye = identity(size)
    square = (size, size)
    basis_red = basis_red_ref[...].reshape(square)
    basis_skel = near_basis[1, 1].reshape(square)
    red_t, skel_t = basis_red.T, basis_skel.T

    kern_inner = wendland(inner_cx, inner_cy, inner_x, inner_y) + eye * noise[:, :size]
    kern_mixed = wendland(inner_cx, inner_cy, cycle_x, cycle_y)
    kern_cycle = wendland(cycle_cx, cycle_cy, cycle_x, cycle_y) + eye * noise[:, size:]
    block = precise(red_t, precise(kern_inner, basis_red))
    mixed = precise(red_t, precise(kern_mixed, basis_skel))
    cycle = precise(skel_t, precise(kern_cycle, basis_skel))
    lower, inverse = factor_block(block)
    rows = precise(inverse, mixed)
    factor[...] = lower
    panel[...] = rows
    schur[...] = cycle - precise(rows.T, rows)

    def finish(n, kind):
        come(n, kind).wait_recv()
        out(n, kind).wait_send()

    for n in range(8):
        each(n, finish)


def flip(index, mask, bit):
    return index + bit * (mask - 2 * mask * (index // mask % 2))


def family(index_x, index_y, p):
    to_x = flip(flip(index_x, 2, p // 8), 1, p // 2 % 2)
    to_y = flip(flip(index_y, 2, p // 4 % 2), 1, p % 2)
    return to_x, to_y


def enter(devices):
    barrier = pltpu.get_barrier_semaphore()
    for device in devices:
        pl.semaphore_signal(barrier, inc=1, device_id=device, device_id_type=pl.DeviceIdType.MESH)
    pl.semaphore_wait(barrier, len(devices))


def coupling_kernel(near_basis, near_shift, schur, couplings, pairs, near, diag, cross, kin, sends, recvs):
    size = near_basis.shape[-1]
    shed = size - size // 4
    index_x, index_y = place()
    child_x, child_y = index_x % 2, index_y % 2
    own_slot = 2 * child_x + child_y
    other_slot = 2 * (1 - child_x) + child_y
    tile_slot = 4 * (2 * (index_x // 2 % 2) + index_y // 2 % 2) + own_slot
    boxes = {p: family(index_x, index_y, p) for p in range(1, 16)}
    enter(list(boxes.values()))
    across = send(schur, diag.at[own_slot], sends.at[0], recvs.at[0], boxes[2])
    beside = send(schur, diag.at[own_slot], sends.at[1], recvs.at[1], boxes[1])
    onward = send(diag.at[other_slot], diag.at[other_slot], sends.at[3], recvs.at[3], boxes[1])
    across_at = (2 - 2 * child_x, 1)
    beside_at = (1, 2 - 2 * child_y)
    relay = send(near_basis.at[across_at], kin.at[other_slot], sends.at[2], recvs.at[2], boxes[1])
    across.start()
    beside.start()
    relay.start()
    kin[2 * (1 - child_x) + child_y] = near_basis[across_at]
    kin[2 * child_x + 1 - child_y] = near_basis[beside_at]
    diag[own_slot] = schur[...]
    table = point_table(size)
    cycle_x, cycle_y = cycle_points(near_shift[1, 1], table)
    column_x, column_y = column(cycle_x), column(cycle_y)
    skel_t = near_basis[1, 1].T

    def couple(n):
        step_x, step_y = OFFSETS[n]
        other_x, other_y = cycle_points(near_shift[1 + step_x, 1 + step_y], table)
        kern = wendland(column_x, column_y, step_x + other_x, step_y + other_y)
        block = precise(skel_t, precise(kern, near_basis[1 + step_x, 1 + step_y]))
        couplings[n] = block
        return block[shed:, shed:]

    tile = jnp.concatenate([couple(n) for n in range(4, 8)], axis=1)
    cross[...] = tile
    near[tile_slot] = tile
    for n in range(2):
        couple(n)
    tiles = [
        send(cross, near.at[tile_slot], sends.at[3 + p], recvs.at[3 + p], boxes[p])
        for p in range(15, 0, -1)
    ]
    for copy in tiles:
        copy.start()
    for n in range(2, 4):
        couple(n)
    across.wait_recv()
    onward.start()
    relay.wait()
    cross_y = child_x * child_y + (1 - child_x) * (1 - child_y)
    mixed_y = 1 - cross_y
    others = (
        ((0, cross_y), (1, 1 - cross_y), 2 + cross_y),
        ((0, 1 - child_y), (1, 1 - child_y), 4 - 3 * child_y),
        ((1 - child_x, 0), (1 - child_x, 1), 5 - 5 * child_x),
    )
    for (low_x, low_y), (high_x, high_y), at in others:
        low_points = cycle_points(near_shift[1 + low_x - child_x, 1 + low_y - child_y], table)
        to_x, to_y = cycle_points(near_shift[1 + high_x - child_x, 1 + high_y - child_y], table)
        step_x = jnp.asarray(high_x - low_x).astype(F32)
        step_y = jnp.asarray(high_y - low_y).astype(F32)
        kern = wendland(column(low_points[0]), column(low_points[1]), step_x + to_x, step_y + to_y)
        basis_t = kin[2 * low_x + low_y].T
        pairs[at] = precise(basis_t, precise(kern, kin[2 * high_x + high_y]))
    mine = (
        (4 - child_y, child_y == 0, 5 * child_x),
        (6 - 5 * child_x, child_x == 0, 1 + 3 * child_y),
        (7 - 5 * child_x - 2 * child_y, child_x == 0, 2 + mixed_y),
    )
    for n, leads, at in mine:
        block = couplings[n]
        pairs[at] = jnp.where(leads, block, block.T)
    across.wait_send()
    for copy in [beside, onward] + tiles:
        copy.wait()


def gather_kernel(schur, diag, sends, recvs, local):
    size = schur.shape[0]
    half = size // 2
    index_x, index_y = place()
    side = index_y % 2
    parent = 2 * (index_x // 2 % 2) + index_y // 2 % 2
    beside = family(index_x, index_y, 1)
    afar = [family(index_x, index_y, p) for p in (12, 8, 4)]
    mine = pltpu.make_async_copy(schur, diag.at[parent], local.at[0])
    mine.start()
    enter([beside] + afar)
    rows = pl.ds(pl.multiple_of(side * half, 8), half)
    out = [
        send(schur.at[rows], diag.at[parent, rows], sends.at[p], recvs.at[p], device)
        for p, device in enumerate(afar)
    ]
    for copy in out:
        copy.start()
    onward = []
    for p in (2, 1, 0):
        other = (
            2 * ((index_x // 2 + (1, 1, 0)[p]) % 2) + (index_y // 2 + (1, 0, 1)[p]) % 2
        )
        out[p].wait_recv()
        block = diag.at[other, rows]
        onward.append(send(block, block, sends.at[3 + p], recvs.at[3 + p], beside))
        onward[-1].start()
    for copy in [mine] + onward:
        copy.wait()
    for copy in out:
        copy.wait_send()


def eliminate_large(shed_rows, kept_block, block, lower, panel_rows):
    size = shed_rows.shape[0]
    work = {
        i: shed_rows[i * block : (i + 1) * block, i * block :] for i in range(size // block)
    }
    for k in range(size // block):
        begin, end = k * block, (k + 1) * block
        factor, inverse = factor_block(work[k][:, :block])
        rest = precise(inverse, work[k][:, block:])
        lower[begin:end, begin:end] = factor
        rest_t = rest.T
        for i in range(k + 1, size // block):
            part_t = rest_t[(i - k - 1) * block : (i - k) * block]
            work[i] = work[i] - precise(part_t, rest[:, (i - k - 1) * block :])
            lower[i * block : (i + 1) * block, begin:end] = part_t
            lower[begin:end, i * block : (i + 1) * block] = jnp.zeros((block, block), F32)
        tail = rest[:, size - end :]
        panel_rows[begin:end] = tail
        kept_block = kept_block - precise(rest_t[size - end :], tail)
    return kept_block


def split_rows(grid, shed):
    top = jnp.concatenate(
        [
            jnp.concatenate([b[:shed, :shed] for b in row] + [b[:shed, shed:] for b in row], axis=1)
            for row in grid
        ],
        axis=0,
    )
    kept = jnp.concatenate(
        [jnp.concatenate([b[shed:, shed:] for b in row], axis=1) for row in grid], axis=0
    )
    return top, kept


def parent_kernel(
    diag, pairs, held_factor, held_panel, held_couplings,
    factor, panel, schur, box_factor, box_panel, couplings,
    lower, panel_rows, local,
):
    out = [
        pltpu.make_async_copy(held_factor, box_factor, local.at[0]),
        pltpu.make_async_copy(held_panel, box_panel, local.at[1]),
        pltpu.make_async_copy(held_couplings, couplings, local.at[2]),
    ]
    for copy in out:
        copy.start()
    size = pairs.shape[-1]
    shed = size - size // 4
    grid = [[None] * 4 for _ in range(4)]
    count = 0
    for slot in range(4):
        grid[slot][slot] = diag[slot]
        for other in range(slot + 1, 4):
            grid[slot][other] = pairs[count]
            grid[other][slot] = pairs[count].T
            count += 1
    rows, kept = split_rows(grid, shed)
    schur[...] = eliminate_large(rows, kept, size, lower, panel_rows)
    index_x, index_y = place()
    own = pl.ds(pl.multiple_of((2 * (index_x % 2) + index_y % 2) * shed, 8), shed)
    factor[...] = lower[own, :]
    panel[...] = panel_rows[own, :]
    for copy in out:
        copy.wait()


def grand_kernel(diag, near, factor, panel, schur, lower, panel_rows, kept_rows):
    size = diag.shape[-1]
    kept_size = size // 4
    shed = size - kept_size
    empty = jnp.zeros((kept_size, kept_size), F32)
    tiles = [near[g] for g in range(16)]
    turned = [tile.T for tile in tiles]

    def piece(e, c, f, d):
        gap_x = 2 * (f // 2 - e // 2) + d // 2 - c // 2
        gap_y = 2 * (f % 2 - e % 2) + d % 2 - c % 2
        if (gap_x, gap_y) in OFFSETS[4:]:
            at = OFFSETS[4:].index((gap_x, gap_y)) * kept_size
            return tiles[4 * e + c][:, at : at + kept_size]
        if (-gap_x, -gap_y) in OFFSETS[4:]:
            at = OFFSETS[4:].index((-gap_x, -gap_y)) * kept_size
            return turned[4 * f + d][at : at + kept_size]
        return empty

    grid = [[None] * 4 for _ in range(4)]
    for e in range(4):
        grid[e][e] = diag[e]
        for f in range(e + 1, 4):
            grid[e][f] = jnp.concatenate(
                [
                    jnp.concatenate([piece(e, c, f, d) for d in range(4)], axis=1)
                    for c in range(4)
                ],
                axis=0,
            )
            grid[f][e] = grid[e][f].T
    rows, kept = split_rows(grid, shed)
    kept_rows[...] = eliminate_large(rows, kept, size, lower, panel_rows)
    index_x, index_y = place()
    parent = 2 * (index_x // 2 % 2) + index_y // 2 % 2
    slot = 4 * parent + 2 * (index_x % 2) + index_y % 2

    def own(count):
        return pl.ds(pl.multiple_of(slot * count, 8), count)

    factor[...] = lower[own(shed // 4), :]
    panel[...] = panel_rows[own(shed // 4), :]
    schur[...] = kept_rows[own(size // 16), :]


def call(body, shapes, args, name, scratch=(), group=None, far=(), out_far=()):
    def spec(far_away):
        return pl.BlockSpec(memory_space=pltpu.HBM if far_away else pltpu.VMEM)

    return pl.pallas_call(
        body,
        out_shape=[jax.ShapeDtypeStruct(s, F32) for s in shapes],
        in_specs=[spec(i in far) for i in range(len(args))],
        out_specs=[spec(i in out_far) for i in range(len(shapes))],
        scratch_shapes=[
            pltpu.SemaphoreType.DMA(s[1:]) if s[0] == 0 else pltpu.VMEM(s, F32) for s in scratch
        ],
        compiler_params=pltpu.CompilerParams(
            vmem_limit_bytes=48 * 2**20,
            collective_id=group,
            has_side_effects=group is not None,
        ),
        name=name,
    )(*args)


def on_device(jitter, noise_var, bases):
    jitter, noise, bases = jitter[0, 0], noise_var[0], bases[0, 0]
    size = bases.shape[-1]
    kept = size // 4
    shed = size - kept
    square = (size, size)
    strips = (8, 2, size // 16, size)
    near_basis, near_shift, held_factor, held_panel, schur = call(
        front_kernel,
        [(3, 3) + strips, (3, 3, 2, size)] + [square] * 3,
        (jitter, noise, bases.reshape((2,) + strips)),
        "front",
        [jitter.shape, noise.shape, strips, (0, 8, 4), (0, 8, 4), (0, 4)],
        group=0,
        far=(0, 1, 2),
    )
    held_couplings, pairs, near, quartet = call(
        coupling_kernel,
        [(8,) + square, (6,) + square, (16, kept, size), (4,) + square],
        (near_basis.reshape((3, 3) + square), near_shift, schur),
        "coupling",
        [(kept, size), (4,) + square, (0, 19), (0, 19)],
        group=1,
    )
    wide = 4 * shed
    parent_factor, parent_panel, parent_schur, factor, panel, couplings = call(
        parent_kernel,
        [(shed, wide), (shed, size), square, square, square, (8,) + square],
        (quartet, pairs, held_factor, held_panel, held_couplings),
        "parent",
        [(wide, wide), (wide, size), (0, 3)],
        out_far=(3, 4, 5),
    )
    (upper,) = call(
        gather_kernel,
        [(4,) + square],
        (parent_schur,),
        "gather",
        [(0, 6), (0, 6), (0, 1)],
        group=2,
    )
    top_factor, top_panel, top_schur = call(
        grand_kernel,
        [(shed // 4, wide), (shed // 4, size), (size // 16, size)],
        (upper, near),
        "grand",
        [(wide, wide), (wide, size), square],
    )
    outs = (
        factor,
        panel,
        couplings,
        parent_factor,
        parent_panel,
        top_factor,
        top_panel,
        top_schur,
    )
    return tuple(value[None, None] for value in outs)


def solution(mesh):
    spec4 = P("bx", "by", None, None)
    spec5 = P("bx", "by", None, None, None)
    return jax.shard_map(
        on_device,
        mesh=mesh,
        in_specs=(spec4, P("bx", "by", None), spec5),
        out_specs=(spec4, spec4, spec5, spec4, spec4, spec4, spec4, spec4),
        check_vma=False,
    )
```
